32 devices in a mesh: grp: 4 (over z), dom: 8 (over y, x, core).
Axes of the slice: x: 2, y: 2, z: 4, core: 2. Of those that a mesh axis runs over, the one named last changes fastest.
Arguments:
- operator_blocks: float32 [128, 16, 4096], P(('grp', 'dom')), may hold values from -0.75 to 0.75
- operator_cols: int32 [128, 16], P(('grp', 'dom')), may hold values from 0 to 15, as said below
- halo_count: int32 [128], P(('grp', 'dom')), may hold values from 2 to 4, as said below
- prolong_blocks: float32 [128, 8, 4096], P(('grp', 'dom')), may hold values from -0.75 to 0.75
- prolong_cols: int32 [128, 8], P(('grp', 'dom')), may hold values from 0 to 63, as said below
- prolong_slot: int32 [128, 8], P(('grp', 'dom')), may hold values from 0 to 15, as said below
- send_lists: int32 [32, 8], P(('grp', 'dom')), may hold values from 0 to 3
- slot_owner_row: int32 [32, 16], P(('grp', 'dom')), may hold values from 0 to 2, as said below
- coarse_pattern: int32 [64, 16], P(('grp', 'dom')), may hold values from 0 to 63, as said below
Outputs:
- coarse_blocks: float32 [64, 16, 4096], P(('grp', 'dom'))
The draws below stay inside these ranges and needn't reach their ends.
Inputs may be any that keep to these rules, and one draw needn't show every extreme that they name: `operator_cols`: slots below 12 hold values below 16, the others values below 8. Slots at or beyond a row's live count hold valid values whose blocks do not count. `halo_count`: the first fine row of every device has 4. `prolong_cols`: the 8 values of a row are different. A row on grp index g names coarse rows owned by devices of grp index g only. Slot t of device v stands for owner dom index t // 2 and owner coarse row slot_owner_row[v, t]; prolong_cols[i, j] = ((v // 8) * 8 + s // 2) * 2 + slot_owner_row[v, s] for s = prolong_slot[i, j]; the slots of a row are different and never empty. `slot_owner_row`: the value 2 marks an empty slot; the live values of one device for one owner are different; every device fills all 2 slots of its own dom index and the first slot of every owner, and no other slot. `coarse_pattern`: the 16 values of a row are different.
All inputs are finite; a program needn't handle non-finite values.
Results may differ from the reference program's by a relative error of at most 0.0003.
Values sent between devices are 32-bit elements; how exact they have to be, the bound alone decides.
A program may use at most 128 MiB of HBM per device.

```python
import jax
import jax.numpy as jnp
from jax import lax

BS = 64
RB = 4
CB = 2
KG = 12
KH = 4
KA = 16
KP = 8
KC = 16
HS = 1
CAP = 2
ROWS = 128
NC = 64
N_GRP = 4
N_DOM = 8


def common_draw(key):
    devices_all = N_GRP * N_DOM
    slot_total = N_DOM * CAP
    far_total = N_DOM * HS
    score = jax.random.randint(jax.random.fold_in(key, 1), (devices_all, N_DOM, CB), 0, 1 << 20) * CB + jnp.arange(CB, dtype=jnp.int32)
    order = jnp.argsort(score, axis=-1)[..., :CAP].astype(jnp.int32)
    own_domain = (jnp.arange(N_DOM, dtype=jnp.int32)[None, :] == (jnp.arange(devices_all, dtype=jnp.int32) % N_DOM)[:, None])[..., None]
    first_slot = (jnp.arange(CAP, dtype=jnp.int32) == 0)[None, None, :]
    live_slot = own_domain | first_slot
    owner_row = jnp.where(live_slot, order, CB).reshape(devices_all, slot_total).astype(jnp.int32)
    live_flat = live_slot.reshape(devices_all, slot_total)
    pick_score = jax.random.randint(jax.random.fold_in(key, 3), (devices_all, RB, slot_total), 0, 1 << 20) * slot_total + jnp.arange(slot_total, dtype=jnp.int32)
    pick_score = jnp.where(live_flat[:, None, :], pick_score, -1)
    chosen = lax.top_k(pick_score, KP)[1].astype(jnp.int32)
    chosen_rows = jnp.take_along_axis(jnp.broadcast_to(owner_row[:, None, :], (devices_all, RB, slot_total)), chosen, axis=2)
    group_of = jnp.arange(devices_all, dtype=jnp.int32) // N_DOM
    prolong_cols = ((group_of[:, None, None] * N_DOM + chosen // CAP) * CB + chosen_rows).reshape(ROWS, KP).astype(jnp.int32)
    prolong_slot = chosen.reshape(ROWS, KP)
    send_lists = jax.random.randint(jax.random.fold_in(key, 4), (devices_all, N_DOM * HS), 0, RB).astype(jnp.int32)
    near_part = jax.random.randint(jax.random.fold_in(key, 5), (ROWS, KG), 0, N_GRP * RB)
    far_score = jax.random.randint(jax.random.fold_in(key, 6), (devices_all, far_total), 0, 1 << 20) * far_total + jnp.arange(far_total, dtype=jnp.int32)
    far_perm = jnp.argsort(far_score, axis=-1).astype(jnp.int32)
    position = (jnp.arange(KH, dtype=jnp.int32)[None, :] * RB + jnp.arange(RB, dtype=jnp.int32)[:, None]) % far_total
    far_part = jnp.take_along_axis(jnp.broadcast_to(far_perm[:, None, :], (devices_all, RB, far_total)), jnp.broadcast_to(position[None], (devices_all, RB, KH)), axis=2).reshape(ROWS, KH)
    operator_cols = jnp.concatenate([near_part, far_part], axis=1).astype(jnp.int32)
    random_count = jax.random.randint(jax.random.fold_in(key, 7), (ROWS,), 2, KH + 1)
    halo_count = jnp.where(jnp.arange(ROWS, dtype=jnp.int32) % RB == 0, KH, random_count).astype(jnp.int32)
    row_index = jnp.arange(ROWS, dtype=jnp.int32)
    device = row_index // RB
    domain = device % N_DOM
    near_rows = (near_part // RB * N_DOM + domain[:, None]) * RB + near_part % RB
    source = (device // N_DOM)[:, None] * N_DOM + far_part // HS
    far_rows = source * RB + send_lists[source, domain[:, None] * HS + far_part % HS]
    columns = jnp.concatenate([near_rows, far_rows], axis=1)
    live_far = (jnp.arange(KH, dtype=jnp.int32)[None, :] < halo_count[:, None]).astype(jnp.int32)
    live_all = jnp.concatenate([jnp.ones((ROWS, KG), jnp.int32), live_far], axis=1)
    expanded = prolong_cols[columns]
    flat_pair = prolong_cols[:, :, None, None] * NC + expanded[:, None, :, :]
    weight_pair = jnp.broadcast_to(live_all[:, None, :, None], flat_pair.shape)
    counts = jnp.zeros((NC * NC,), jnp.int32).at[flat_pair.reshape(-1)].add(weight_pair.reshape(-1)).reshape(NC, NC)
    tie_break = jax.random.randint(jax.random.fold_in(key, 8), (NC, NC), 0, 1 << 10) * NC + jnp.arange(NC, dtype=jnp.int32)[None, :]
    coarse_pattern = lax.top_k(counts * (NC << 10) + tie_break, KC)[1].astype(jnp.int32)
    return (operator_cols, halo_count, prolong_cols, prolong_slot, send_lists, owner_row, coarse_pattern)


def draw_operator_cols(key, part):
    return common_draw(jax.random.fold_in(key, 77))[0]


def draw_halo_count(key, part):
    return common_draw(jax.random.fold_in(key, 77))[1]


def draw_prolong_cols(key, part):
    return common_draw(jax.random.fold_in(key, 77))[2]


def draw_prolong_slot(key, part):
    return common_draw(jax.random.fold_in(key, 77))[3]


def draw_send_lists(key, part):
    return common_draw(jax.random.fold_in(key, 77))[4]


def draw_slot_owner_row(key, part):
    return common_draw(jax.random.fold_in(key, 77))[5]


def draw_coarse_pattern(key, part):
    return common_draw(jax.random.fold_in(key, 77))[6]


def level_of(stream_key, shape, split, low, largest):
    loudness = 1.0
    for dim, parts in split:
        draws = jax.random.uniform(jax.random.fold_in(jax.random.fold_in(stream_key, 6), dim), (parts,), jnp.float32, low / len(split), largest / len(split))
        loudness = loudness * jnp.repeat(jnp.exp(draws), shape[dim] // parts).reshape((-1,) + (1,) * (len(shape) - 1 - dim))
    return loudness


def scatter_about(stream_key, shape, spread, bound, split=(), held_as=jnp.bfloat16):
    array = jax.random.normal(stream_key, shape, jnp.float32) * spread
    if len(split) > 0:
        array = level_of(stream_key, shape, split, -0.22, 0.18) * array
    return jnp.clip(array, min=-bound, max=bound).astype(held_as)


def setup_inputs(seed: int = 0) -> dict:
    splits = jax.random.split(jax.random.key(seed), 10)
    return {
        "operator_blocks": scatter_about(splits[0], (ROWS, KA, BS * BS), BS ** -0.5, 0.75, ((0, 32),), jnp.float32),
        "operator_cols": draw_operator_cols(jax.random.fold_in(splits[9], 71), 0),
        "halo_count": draw_halo_count(jax.random.fold_in(splits[9], 71), 0),
        "prolong_blocks": scatter_about(splits[3], (ROWS, KP, BS * BS), BS ** -0.5, 0.75, ((0, 32),), jnp.float32),
        "prolong_cols": draw_prolong_cols(jax.random.fold_in(splits[9], 71), 0),
        "prolong_slot": draw_prolong_slot(jax.random.fold_in(splits[9], 71), 0),
        "send_lists": draw_send_lists(jax.random.fold_in(splits[9], 71), 0),
        "slot_owner_row": draw_slot_owner_row(jax.random.fold_in(splits[9], 71), 0),
        "coarse_pattern": draw_coarse_pattern(jax.random.fold_in(splits[9], 71), 0),
    }


EXACT = lax.Precision.HIGHEST


def column_map(operator_cols, send_lists):
    row_index = jnp.arange(ROWS, dtype=jnp.int32)
    device = row_index // RB
    group_index = device // N_DOM
    domain = device % N_DOM
    near_slots = operator_cols[:, :KG]
    near_rows = ((near_slots // RB) * N_DOM + domain[:, None]) * RB + near_slots % RB
    far_slots = operator_cols[:, KG:]
    source = group_index[:, None] * N_DOM + far_slots // HS
    far_rows = source * RB + send_lists[source, domain[:, None] * HS + far_slots % HS]
    return jnp.concatenate([near_rows, far_rows], axis=1).astype(jnp.int32)


def live_mask(halo_count):
    near_live = jnp.ones((halo_count.shape[0], KG), jnp.float32)
    far_live = (jnp.arange(KH, dtype=jnp.int32)[None, :] < halo_count[:, None]).astype(jnp.float32)
    return jnp.concatenate([near_live, far_live], axis=1)


def target_rows(prolong_slot, slot_owner_row):
    device = jnp.arange(ROWS, dtype=jnp.int32) // RB
    owner_row = slot_owner_row[device[:, None], prolong_slot]
    return (((device // N_DOM)[:, None] * N_DOM + prolong_slot // CAP) * CB + owner_row).astype(jnp.int32)


def reference(operator_blocks, operator_cols, halo_count, prolong_blocks, prolong_cols, prolong_slot, send_lists, slot_owner_row, coarse_pattern):
    columns = column_map(operator_cols, send_lists)
    live_slots = jnp.repeat(live_mask(halo_count), KP, axis=1)
    expanded_ids = prolong_cols[columns].reshape(ROWS, KA * KP)
    target_ids = target_rows(prolong_slot, slot_owner_row)
    block_count = ROWS // RB
    square = prolong_blocks.reshape(ROWS, KP, BS, BS)
    blocks = (operator_blocks.reshape(block_count, RB, KA, BS, BS), columns.reshape(block_count, RB, KA),
              expanded_ids.reshape(block_count, RB, KA * KP), live_slots.reshape(block_count, RB, KA * KP),
              square.reshape(block_count, RB, KP, BS, BS), target_ids.reshape(block_count, RB, KP))

    def add_block(coarse_sum, pieces):
        operator, columns_block, coarse_ids, live_block, panels, targets = pieces
        fetched = square[columns_block]
        weights = jnp.einsum('rmax,rmqxd->rmqad', operator, fetched, precision=EXACT).reshape(RB, KA * KP, BS * BS)
        wanted = coarse_pattern[targets]
        select = (wanted[..., None] == coarse_ids[:, None, None, :]).astype(jnp.float32) * live_block[:, None, None, :]
        matched = jnp.einsum('rjce,rex->rjcx', select, weights, precision=EXACT).reshape(RB, KP, KC, BS, BS)
        pair_terms = jnp.einsum('rjab,rjcad->rjcbd', panels, matched, precision=EXACT)
        return coarse_sum.at[targets.reshape(RB * KP)].add(pair_terms.reshape(RB * KP, KC, BS * BS)), None

    start = jnp.zeros((NC, KC, BS * BS), jnp.float32)
    return lax.scan(add_block, start, blocks)[0]
```

```python
import functools

import jax
import jax.numpy as jnp
from jax import lax
from jax.experimental import pallas as pl
from jax.experimental.pallas import tpu as pltpu
from jax.sharding import PartitionSpec as P

BS = 64
KG = 12
KH = 4
LANES = 128


def any_spec():
    return pl.BlockSpec(memory_space=pl.ANY)


def vmem_spec():
    return pl.BlockSpec(memory_space=pltpu.VMEM)


def smem_spec():
    return pl.BlockSpec(memory_space=pltpu.SMEM)


def gather_kernel(
    n_grp, n_dom, rows, hs,
    panels, outgoing, dom_meta, grp_meta,
    table, meta,
    own_sem, line_send, line_recv, dom_send, dom_recv, meta_send, meta_recv,
):
    g = lax.axis_index("grp")
    me = lax.axis_index("dom")
    far_base = n_grp * rows
    barrier = pltpu.get_barrier_semaphore()
    for k in range(1, n_grp):
        pl.semaphore_signal(barrier, inc=1, device_id={"grp": lax.rem(g + k, n_grp)})
    for k in range(1, n_dom):
        pl.semaphore_signal(barrier, inc=1, device_id={"dom": lax.rem(me + k, n_dom)})
    pl.semaphore_wait(barrier, n_grp + n_dom - 2)

    def line_copy(direction, step, r, src, origin):
        target = g + 1 if direction == 0 else g - 1
        return pltpu.make_async_remote_copy(
            src_ref=src,
            dst_ref=table.at[origin * rows + r],
            send_sem=line_send.at[direction, step, r],
            recv_sem=line_recv.at[direction, step, r],
            device_id={"grp": target},
        )

    can_send = (g < n_grp - 1, g > 0)
    for r in range(rows):
        for direction in range(2):
            @pl.when(can_send[direction])
            def _():
                line_copy(direction, 0, r, panels.at[r], g).start()

    def meta_copy(k, over_dom):
        if over_dom:
            target = lax.rem(me + k, n_dom)
            return pltpu.make_async_remote_copy(
                src_ref=dom_meta.at[target], dst_ref=meta.at[n_grp + me],
                send_sem=meta_send.at[n_grp + k], recv_sem=meta_recv.at[n_grp + k],
                device_id={"dom": target},
            )
        return pltpu.make_async_remote_copy(
            src_ref=grp_meta, dst_ref=meta.at[g],
            send_sem=meta_send.at[k], recv_sem=meta_recv.at[k],
            device_id={"grp": lax.rem(g + k, n_grp)},
        )

    def dom_copy(k):
        target = lax.rem(me + k, n_dom)
        return pltpu.make_async_remote_copy(
            src_ref=outgoing.at[pl.ds(target * hs, hs)],
            dst_ref=table.at[pl.ds(far_base + me * hs, hs)],
            send_sem=dom_send.at[k], recv_sem=dom_recv.at[k],
            device_id={"dom": target},
        )

    for k in range(1, n_grp):
        meta_copy(k, False).start()
    for k in range(1, n_dom):
        dom_copy(k).start()
        meta_copy(k, True).start()
    own = (
        pltpu.make_async_copy(panels, table.at[pl.ds(g * rows, rows)], own_sem.at[0]),
        pltpu.make_async_copy(outgoing.at[pl.ds(me * hs, hs)], table.at[pl.ds(far_base + me * hs, hs)], own_sem.at[1]),
        pltpu.make_async_copy(grp_meta, meta.at[g], own_sem.at[2]),
        pltpu.make_async_copy(dom_meta.at[me], meta.at[n_grp + me], own_sem.at[3]),
    )
    for copy in own:
        copy.start()

    def origin_of(direction, step):
        return g - 1 - step if direction == 0 else g + 1 + step

    for step in range(n_grp - 1):
        for r in range(rows):
            for direction in range(2):
                origin = origin_of(direction, step)
                exists = (origin >= 0) & (origin < n_grp)

                @pl.when(exists)
                def _():
                    src = table.at[origin * rows + r]
                    line_copy(direction, step, r, src, origin).wait_recv()

                if step < n_grp - 2:
                    @pl.when(exists & can_send[direction])
                    def _():
                        src = table.at[origin * rows + r]
                        line_copy(direction, step + 1, r, src, origin).start()

    for copy in own:
        copy.wait()
    for k in range(1, n_grp):
        meta_copy(k, False).wait()
    for k in range(1, n_dom):
        dom_copy(k).wait()
        meta_copy(k, True).wait()
    for step in range(n_grp - 1):
        for r in range(rows):
            for direction in range(2):
                origin = g - step if direction == 0 else g + step
                exists = (origin >= 0) & (origin < n_grp)

                @pl.when(exists & can_send[direction])
                def _():
                    line_copy(direction, step, r, panels.at[r], origin).wait_send()


def split_pair(x):
    high = x.astype(jnp.bfloat16)
    low = (x - high.astype(jnp.float32)).astype(jnp.bfloat16)
    return high, low


def product_kernel(
    n_grp, n_dom, rows, hs, ka, kp, kc, cap,
    cols, halo, slots, owner, meta,
    operator, table, prolong,
    out,
    split_table, total,
):
    k = pl.program_id(0)
    me = lax.axis_index("dom")
    panel_count = table.shape[0]
    near_count = n_grp * rows
    lane = lax.broadcasted_iota(jnp.int32, (BS, LANES), 1) < BS

    @pl.when(k == 0)
    def _():
        def clear(e, carry):
            total[e] = jnp.zeros(total.shape[1:], jnp.float32)
            return carry

        lax.fori_loop(0, total.shape[0], clear, 0)

        def split(p, carry):
            high, low = split_pair(table[p])
            split_table[p, 0:BS] = high
            split_table[p, BS:2 * BS] = low
            split_table[p, 2 * BS:3 * BS] = high
            return carry

        lax.fori_loop(0, panel_count, split, 0)

        def pair(step, carry):
            i = step // ka
            m = step % ka
            col = cols[i, m]
            near = m < KG

            @pl.when(near | (m - KG < halo[i]))
            def _():
                panel = jnp.where(near, col, near_count + col)
                meta_row = jnp.where(near, col // rows, n_grp + col // hs)
                meta_lane = jnp.where(near, (col % rows) * kp, (col % hs) * kp)
                high, low = split_pair(operator[i, m])
                high = high.astype(jnp.float32)
                low = low.astype(jnp.float32)
                left = jnp.concatenate([high, high, low], axis=1).astype(jnp.bfloat16)
                w = jnp.dot(left, split_table[panel], preferred_element_type=jnp.float32)
                for q in range(0, kp, 2):
                    piece = w[:, q * BS:(q + 2) * BS]
                    first = meta[meta_row, meta_lane + q]
                    second = meta[meta_row, meta_lane + q + 1]
                    total[first, i] += jnp.where(lane, piece, 0.0)
                    total[second, i] += jnp.where(lane, 0.0, piece)

            return carry

        lax.fori_loop(0, rows * ka, pair, 0)

    own_extra = k >= n_dom
    owner_dom = jnp.where(own_extra, me, k)
    slot = jnp.where(own_extra, me * cap + 1 + k - n_dom, k * cap)
    owner_row = owner[slot]
    pattern_at = hs * kp + owner_row * kc
    left = []
    for i in range(rows):
        place = jnp.int32(kp)
        for j in range(kp):
            place = jnp.where(slots[i, j] == slot, j, place)
        block = prolong[i, jnp.minimum(place, kp - 1)]
        left.append(jnp.where(place < kp, block, 0.0).T)
    left = jnp.concatenate(left, axis=1)
    left_high, left_low = split_pair(left)
    both = jnp.concatenate([left_high, left_low], axis=0)
    wide = lax.broadcasted_iota(jnp.int32, (rows, BS, LANES), 2) < BS
    for c in range(0, kc, 4):
        highs = []
        lows = []
        for h in range(2):
            first = total[meta[n_grp + owner_dom, pattern_at + c + 2 * h]]
            second = total[meta[n_grp + owner_dom, pattern_at + c + 2 * h + 1]]
            kept = jnp.where(wide, first, second).reshape(rows * BS, LANES)
            turned = pltpu.roll(jnp.where(wide, second, first).reshape(rows * BS, LANES), BS, 1)
            high, low = split_pair(kept + turned)
            highs.append(high)
            lows.append(low)
        high = jnp.concatenate(highs, axis=1)
        low = jnp.concatenate(lows, axis=1)
        stacked = jnp.dot(both, high, preferred_element_type=jnp.float32)
        rest = jnp.dot(left_high, low, preferred_element_type=jnp.float32)
        out[0, :, c * BS:(c + 4) * BS] = stacked[:BS] + stacked[BS:] + rest


def reduce_kernel(
    n_grp, n_dom, cap, row_at,
    owner, meta, partial,
    out,
    arrived, send_sem, recv_sem,
):
    me = lax.axis_index("dom")
    barrier = pltpu.get_barrier_semaphore()
    for k in range(1, n_dom):
        pl.semaphore_signal(barrier, inc=1, device_id={"dom": lax.rem(me + k, n_dom)})
    pl.semaphore_wait(barrier, n_dom - 1)

    def copy_of(k):
        target = lax.rem(me + k, n_dom)
        return pltpu.make_async_remote_copy(
            src_ref=partial.at[target], dst_ref=arrived.at[k - 1],
            send_sem=send_sem.at[k - 1], recv_sem=recv_sem.at[k - 1],
            device_id={"dom": target},
        )

    for k in range(1, n_dom):
        copy_of(k).start()
    owned = out.shape[0]
    for r in range(owned):
        value = partial[me] * (owner[me * cap] == r).astype(jnp.float32)
        for t in range(1, cap):
            value += partial[n_dom + t - 1] * (owner[me * cap + t] == r).astype(jnp.float32)
        out[r] = value
    for k in range(1, n_dom):
        copy_of(k).wait_recv()
        source = lax.rem(me - k + n_dom, n_dom)
        row = meta[n_grp + source, row_at]
        for r in range(owned):
            out[r] += arrived[k - 1] * (row == r).astype(jnp.float32)
    for k in range(1, n_dom):
        copy_of(k).wait_send()


def per_device(
    operator_blocks, operator_cols, halo_count, prolong_blocks, prolong_cols,
    prolong_slot, send_lists, slot_owner_row, coarse_pattern,
):
    n_grp = lax.axis_size("grp")
    n_dom = lax.axis_size("dom")
    rows, ka = operator_cols.shape
    kp = prolong_cols.shape[1]
    owned, kc = coarse_pattern.shape
    hs = send_lists.shape[1] // n_dom
    cap = slot_owner_row.shape[1] // n_dom
    owner = slot_owner_row.reshape(n_dom * cap)
    total_ids = owned * n_grp * n_dom
    used = n_dom + cap - 1
    panel_count = n_grp * rows + n_dom * hs

    prolong = prolong_blocks.reshape(rows, kp, BS, BS)
    panels = prolong.transpose(0, 2, 1, 3).reshape(rows, BS, kp * BS)
    picked = send_lists.reshape(n_dom * hs)
    outgoing = jnp.take(panels, picked, axis=0, mode="clip")
    grp_meta = jnp.pad(prolong_cols.reshape(1, rows * kp), ((0, 0), (0, LANES - rows * kp)))
    row_at = hs * kp + owned * kc
    dom_meta = jnp.concatenate(
        [
            jnp.take(prolong_cols, picked, axis=0, mode="clip").reshape(n_dom, hs * kp),
            jnp.broadcast_to(coarse_pattern.reshape(1, owned * kc), (n_dom, owned * kc)),
            owner.reshape(n_dom, cap)[:, :1],
            jnp.zeros((n_dom, LANES - row_at - 1), jnp.int32),
        ],
        axis=1,
    ).reshape(n_dom, 1, LANES)

    sem = pltpu.SemaphoreType.DMA
    table, meta = pl.pallas_call(
        functools.partial(gather_kernel, n_grp, n_dom, rows, hs),
        out_shape=(
            jax.ShapeDtypeStruct((panel_count, BS, kp * BS), jnp.float32),
            jax.ShapeDtypeStruct((n_grp + n_dom, 1, LANES), jnp.int32),
        ),
        in_specs=[vmem_spec()] * 4,
        out_specs=(any_spec(), any_spec()),
        scratch_shapes=[
            sem((4,)), sem((2, n_grp - 1, rows)), sem((2, n_grp - 1, rows)),
            sem((n_dom,)), sem((n_dom,)), sem((n_grp + n_dom,)), sem((n_grp + n_dom,)),
        ],
        compiler_params=pltpu.CompilerParams(collective_id=0, has_side_effects=True),
        name="gather_rows",
    )(panels, outgoing, dom_meta, grp_meta)
    meta = meta.reshape(n_grp + n_dom, LANES)

    whole = lambda shape: pl.BlockSpec(shape, lambda k: (0,) * len(shape), pipeline_mode=pl.Buffered(1))
    partial = pl.pallas_call(
        functools.partial(product_kernel, n_grp, n_dom, rows, hs, ka, kp, kc, cap),
        grid=(used,),
        out_shape=jax.ShapeDtypeStruct((used, BS, kc * BS), jnp.float32),
        in_specs=[smem_spec()] * 5 + [
            whole((rows, ka, BS, BS)), whole((panel_count, BS, kp * BS)), whole((rows, kp, BS, BS)),
        ],
        out_specs=pl.BlockSpec((1, BS, kc * BS), lambda k: (k, 0, 0)),
        scratch_shapes=[
            pltpu.VMEM((panel_count, 3 * BS, kp * BS), jnp.bfloat16),
            pltpu.VMEM((total_ids, rows, BS, LANES), jnp.float32),
        ],
        compiler_params=pltpu.CompilerParams(vmem_limit_bytes=63000 * 1024),
        name="block_products",
    )(
        operator_cols, halo_count, prolong_slot, owner, meta,
        operator_blocks.reshape(rows, ka, BS, BS), table, prolong,
    )

    summed = pl.pallas_call(
        functools.partial(reduce_kernel, n_grp, n_dom, cap, row_at),
        out_shape=jax.ShapeDtypeStruct((owned, BS, kc * BS), jnp.float32),
        in_specs=[smem_spec(), smem_spec(), vmem_spec()],
        out_specs=vmem_spec(),
        scratch_shapes=[
            pltpu.VMEM((n_dom - 1, BS, kc * BS), jnp.float32),
            sem((n_dom - 1,)), sem((n_dom - 1,)),
        ],
        compiler_params=pltpu.CompilerParams(collective_id=1, has_side_effects=True),
        name="sum_rows",
    )(owner, meta, partial)
    return summed.reshape(owned, BS, kc, BS).transpose(0, 2, 1, 3).reshape(owned, kc, BS * BS)


def solution(mesh):
    blocks = P(("grp", "dom"), None, None)
    lists = P(("grp", "dom"), None)
    return jax.shard_map(
        per_device,
        mesh=mesh,
        in_specs=(blocks, lists, P(("grp", "dom")), blocks, lists, lists, lists, lists, lists),
        out_specs=blocks,
        check_vma=False,
    )
```

```python
import functools

import jax
import jax.numpy as jnp
from jax import lax
from jax.experimental import pallas as pl
from jax.experimental.pallas import tpu as pltpu
from jax.sharding import PartitionSpec as P

BS = 64
KG = 12
KH = 4
LANES = 128


def any_spec():
    return pl.BlockSpec(memory_space=pl.ANY)


def vmem_spec():
    return pl.BlockSpec(memory_space=pltpu.VMEM)


def smem_spec():
    return pl.BlockSpec(memory_space=pltpu.SMEM)


def gather_kernel(
    n_grp, n_dom, rows, hs,
    panels, outgoing, dom_meta, grp_meta, operator,
    table, meta, blocks,
    own_sem, line_send, line_recv, dom_send, dom_recv, meta_send, meta_recv,
):
    g = lax.axis_index("grp")
    me = lax.axis_index("dom")
    far_base = n_grp * rows
    barrier = pltpu.get_barrier_semaphore()
    for k in range(1, n_grp):
        pl.semaphore_signal(barrier, inc=1, device_id={"grp": lax.rem(g + k, n_grp)})
    for k in range(1, n_dom):
        pl.semaphore_signal(barrier, inc=1, device_id={"dom": lax.rem(me + k, n_dom)})
    pl.semaphore_wait(barrier, n_grp + n_dom - 2)

    def line_copy(direction, step, r, src, origin):
        target = g + 1 if direction == 0 else g - 1
        return pltpu.make_async_remote_copy(
            src_ref=src,
            dst_ref=table.at[origin * rows + r],
            send_sem=line_send.at[direction, step, r],
            recv_sem=line_recv.at[direction, step, r],
            device_id={"grp": target},
        )

    can_send = (g < n_grp - 1, g > 0)
    for r in range(rows):
        for direction in range(2):
            @pl.when(can_send[direction])
            def _():
                line_copy(direction, 0, r, panels.at[r], g).start()

    def meta_copy(k, over_dom):
        if over_dom:
            target = lax.rem(me + k, n_dom)
            return pltpu.make_async_remote_copy(
                src_ref=dom_meta.at[target], dst_ref=meta.at[n_grp + me],
                send_sem=meta_send.at[n_grp + k], recv_sem=meta_recv.at[n_grp + k],
                device_id={"dom": target},
            )
        return pltpu.make_async_remote_copy(
            src_ref=grp_meta, dst_ref=meta.at[g],
            send_sem=meta_send.at[k], recv_sem=meta_recv.at[k],
            device_id={"grp": lax.rem(g + k, n_grp)},
        )

    def dom_copy(k):
        target = lax.rem(me + k, n_dom)
        return pltpu.make_async_remote_copy(
            src_ref=outgoing.at[pl.ds(target * hs, hs)],
            dst_ref=table.at[pl.ds(far_base + me * hs, hs)],
            send_sem=dom_send.at[k], recv_sem=dom_recv.at[k],
            device_id={"dom": target},
        )

    for k in range(1, n_grp):
        meta_copy(k, False).start()
    for k in range(1, n_dom):
        dom_copy(k).start()
        meta_copy(k, True).start()
    own = (
        pltpu.make_async_copy(panels, table.at[pl.ds(g * rows, rows)], own_sem.at[0]),
        pltpu.make_async_copy(outgoing.at[pl.ds(me * hs, hs)], table.at[pl.ds(far_base + me * hs, hs)], own_sem.at[1]),
        pltpu.make_async_copy(grp_meta, meta.at[g], own_sem.at[2]),
        pltpu.make_async_copy(dom_meta.at[me], meta.at[n_grp + me], own_sem.at[3]),
    )
    for copy in own:
        copy.start()

    def relay_row(i, carry):
        row = operator[i]
        for a in range(BS):
            blocks[i, :, a, :] = row[:, a * BS:(a + 1) * BS]
        return carry

    lax.fori_loop(0, rows, relay_row, 0)

    def origin_of(direction, step):
        return g - 1 - step if direction == 0 else g + 1 + step

    for step in range(n_grp - 1):
        for r in range(rows):
            for direction in range(2):
                origin = origin_of(direction, step)
                exists = (origin >= 0) & (origin < n_grp)

                @pl.when(exists)
                def _():
                    src = table.at[origin * rows + r]
                    line_copy(direction, step, r, src, origin).wait_recv()

                if step < n_grp - 2:
                    @pl.when(exists & can_send[direction])
                    def _():
                        src = table.at[origin * rows + r]
                        line_copy(direction, step + 1, r, src, origin).start()

    for copy in own:
        copy.wait()
    for k in range(1, n_grp):
        meta_copy(k, False).wait()
    for k in range(1, n_dom):
        dom_copy(k).wait()
        meta_copy(k, True).wait()
    for step in range(n_grp - 1):
        for r in range(rows):
            for direction in range(2):
                origin = g - step if direction == 0 else g + step
                exists = (origin >= 0) & (origin < n_grp)

                @pl.when(exists & can_send[direction])
                def _():
                    line_copy(direction, step, r, panels.at[r], origin).wait_send()


def split_pair(x):
    high = x.astype(jnp.bfloat16)
    low = (x - high.astype(jnp.float32)).astype(jnp.bfloat16)
    return high, low


def product_kernel(
    n_grp, n_dom, rows, hs, ka, kp,
    cols, halo, meta,
    operator, table,
    out,
    split_table, total,
):
    k = pl.program_id(0)
    panel_count = table.shape[0]
    near_count = n_grp * rows
    lane = lax.broadcasted_iota(jnp.int32, (BS, LANES), 1) < BS

    @pl.when(k == 0)
    def _():
        def clear(e, carry):
            total[e] = jnp.zeros(total.shape[1:], jnp.float32)
            return carry

        lax.fori_loop(0, total.shape[0], clear, 0)

        def split(p, carry):
            high, low = split_pair(table[p])
            split_table[p, 0:BS] = high
            split_table[p, BS:2 * BS] = low
            split_table[p, 2 * BS:3 * BS] = high
            return carry

        lax.fori_loop(0, panel_count, split, 0)

        def pair(step, carry):
            i = step // ka
            m = step % ka
            col = cols[i, m]
            near = m < KG

            @pl.when(near | (m - KG < halo[i]))
            def _():
                panel = jnp.where(near, col, near_count + col)
                meta_row = jnp.where(near, col // rows, n_grp + col // hs)
                meta_lane = jnp.where(near, (col % rows) * kp, (col % hs) * kp)
                high, low = split_pair(operator[i, m])
                high = high.astype(jnp.float32)
                low = low.astype(jnp.float32)
                left = jnp.concatenate([high, high, low], axis=1).astype(jnp.bfloat16)
                w = jnp.dot(left, split_table[panel], preferred_element_type=jnp.float32)
                for q in range(0, kp, 2):
                    piece = w[:, q * BS:(q + 2) * BS]
                    first = meta[meta_row, meta_lane + q]
                    second = meta[meta_row, meta_lane + q + 1]
                    total[first, i] += jnp.where(lane, piece, 0.0)
                    total[second, i] += jnp.where(lane, 0.0, piece)

            return carry

        lax.fori_loop(0, rows * ka, pair, 0)

    chunk = out.shape[0]
    half = lax.broadcasted_iota(jnp.int32, (rows * BS, LANES), 1) < BS

    def fold(t, carry):
        value = total[k * chunk + t].reshape(rows * BS, LANES)
        value += pltpu.roll(value, BS, 1)
        high = value.astype(jnp.bfloat16).astype(jnp.float32)
        out[t] = jnp.where(half, high, value - high).astype(jnp.bfloat16)
        return carry

    lax.fori_loop(0, chunk, fold, 0)


def exchange_kernel(
    n_grp, n_dom, rows, hs, kp, kc, cap, row_at,
    slots, owner, meta, packed, prolong,
    out,
    partial, arrived, send_sem, recv_sem,
):
    me = lax.axis_index("dom")
    barrier = pltpu.get_barrier_semaphore()
    for k in range(1, n_dom):
        pl.semaphore_signal(barrier, inc=1, device_id={"dom": lax.rem(me + k, n_dom)})
    pl.semaphore_wait(barrier, n_dom - 1)
    lane = lax.broadcasted_iota(jnp.int32, (BS, LANES), 1) < BS

    def slot_rows(owner_dom, slot, at):
        owner_row = owner[0, slot]
        pattern_at = hs * kp + owner_row * kc
        left = []
        for i in range(rows):
            place = jnp.int32(kp)
            for j in range(kp):
                place = jnp.where(slots[i, j] == slot, j, place)
            block = prolong[i, jnp.minimum(place, kp - 1)]
            left.append(jnp.where(place < kp, block, 0.0).T)
        left_high, left_low = split_pair(jnp.concatenate(left, axis=1))
        both = jnp.concatenate([left_high, left_low], axis=0)
        for c in range(0, kc, 2):
            right = jnp.concatenate(
                [packed[meta[n_grp + owner_dom, pattern_at + c + h]] for h in range(2)], axis=1
            )
            stacked = jnp.dot(both, right, preferred_element_type=jnp.float32)
            both_sum = stacked[:BS] + stacked[BS:]
            folded = []
            for h in range(2):
                piece = both_sum[:, h * LANES:(h + 1) * LANES]
                folded.append(piece + pltpu.roll(piece, BS, 1))
            partial[at, :, c * BS:(c + 2) * BS] = jnp.where(lane, folded[0], folded[1])

    def copy_of(k):
        target = lax.rem(me + k, n_dom)
        return pltpu.make_async_remote_copy(
            src_ref=partial.at[k], dst_ref=arrived.at[k - 1],
            send_sem=send_sem.at[k - 1], recv_sem=recv_sem.at[k - 1],
            device_id={"dom": target},
        )

    def far_slot(k, carry):
        target = lax.rem(me + k, n_dom)
        slot_rows(target, target * cap, k)

        @pl.when(k > 1)
        def _():
            copy_of(k - 1).start()

        return carry

    lax.fori_loop(1, n_dom, far_slot, 0)
    slot_rows(me, me * cap, 0)
    copy_of(n_dom - 1).start()
    owned = out.shape[0]
    for r in range(owned):
        out[r] = partial[0] * (owner[0, me * cap] == r).astype(jnp.float32)
    for t in range(1, cap):
        slot_rows(me, me * cap + t, n_dom + t - 1)
        for r in range(owned):
            out[r] += partial[n_dom + t - 1] * (owner[0, me * cap + t] == r).astype(jnp.float32)
    for k in range(1, n_dom):
        copy_of(k).wait_recv()
        source = lax.rem(me - k + n_dom, n_dom)
        row = meta[n_grp + source, row_at]
        for r in range(owned):
            out[r] += arrived[k - 1] * (row == r).astype(jnp.float32)
    for k in range(1, n_dom):
        copy_of(k).wait_send()


def prepare_kernel(
    n_dom, rows, hs, kp, kc, cap,
    picked, owner, prolong_raw, prolong_cols, pattern,
    panels, outgoing, prolong, dom_meta, grp_meta,
):
    owned = pattern.shape[0]
    for i in range(rows):
        raw = prolong_raw[i]
        for a in range(BS):
            prolong[i, :, a, :] = raw[:, a * BS:(a + 1) * BS]
        for q in range(0, kp, 2):
            panels[i, :, q * BS:(q + 2) * BS] = jnp.concatenate([prolong[i, q], prolong[i, q + 1]], axis=1)
    grp_meta[...] = jnp.zeros(grp_meta.shape, jnp.int32)
    dom_meta[...] = jnp.zeros(dom_meta.shape, jnp.int32)
    for i in range(rows):
        grp_meta[:, i * kp:(i + 1) * kp] = prolong_cols[i:i + 1, :]
    row_at = hs * kp + owned * kc

    def for_dom(d, carry):
        for h in range(hs):
            row = picked[0, d * hs + h]
            outgoing[d * hs + h] = panels[row]
            dom_meta[d, :, h * kp:(h + 1) * kp] = prolong_cols[pl.ds(row, 1), :]
        for r in range(owned):
            at = hs * kp + r * kc
            dom_meta[d, :, at:at + kc] = pattern[r:r + 1, :]
        dom_meta[d, :, row_at:row_at + 1] = jnp.full((1, 1), owner[0, d * cap], jnp.int32)
        return carry

    lax.fori_loop(0, n_dom, for_dom, 0)


def per_device(
    operator_blocks, operator_cols, halo_count, prolong_blocks, prolong_cols,
    prolong_slot, send_lists, slot_owner_row, coarse_pattern,
):
    n_grp = lax.axis_size("grp")
    n_dom = lax.axis_size("dom")
    rows, ka = operator_cols.shape
    kp = prolong_cols.shape[1]
    owned, kc = coarse_pattern.shape
    hs = send_lists.shape[1] // n_dom
    cap = slot_owner_row.shape[1] // n_dom
    total_ids = owned * n_grp * n_dom
    used = n_dom + cap - 1
    panel_count = n_grp * rows + n_dom * hs
    row_at = hs * kp + owned * kc
    f32 = lambda *shape: jax.ShapeDtypeStruct(shape, jnp.float32)
    i32 = lambda *shape: jax.ShapeDtypeStruct(shape, jnp.int32)

    panels, outgoing, prolong, dom_meta, grp_meta = pl.pallas_call(
        functools.partial(prepare_kernel, n_dom, rows, hs, kp, kc, cap),
        out_shape=(
            f32(rows, BS, kp * BS), f32(n_dom * hs, BS, kp * BS), f32(rows, kp, BS, BS),
            i32(n_dom, 1, LANES), i32(1, LANES),
        ),
        in_specs=[smem_spec()] * 2 + [vmem_spec()] * 3,
        out_specs=(vmem_spec(),) * 5,
        name="prepare",
    )(send_lists, slot_owner_row, prolong_blocks, prolong_cols, coarse_pattern)

    sem = pltpu.SemaphoreType.DMA
    table, meta, blocks = pl.pallas_call(
        functools.partial(gather_kernel, n_grp, n_dom, rows, hs),
        out_shape=(
            f32(panel_count, BS, kp * BS), i32(n_grp + n_dom, 1, LANES), f32(rows, ka, BS, BS),
        ),
        in_specs=[vmem_spec()] * 5,
        out_specs=(any_spec(), any_spec(), vmem_spec()),
        scratch_shapes=[
            sem((4,)), sem((2, n_grp - 1, rows)), sem((2, n_grp - 1, rows)),
            sem((n_dom,)), sem((n_dom,)), sem((n_grp + n_dom,)), sem((n_grp + n_dom,)),
        ],
        compiler_params=pltpu.CompilerParams(collective_id=0, has_side_effects=True),
        name="gather_rows",
    )(panels, outgoing, dom_meta, grp_meta, operator_blocks)
    meta = meta.reshape(n_grp + n_dom, LANES)

    whole = lambda shape: pl.BlockSpec(shape, lambda k: (0,) * len(shape), pipeline_mode=pl.Buffered(1))
    chunk = 8
    packed = pl.pallas_call(
        functools.partial(product_kernel, n_grp, n_dom, rows, hs, ka, kp),
        grid=(total_ids // chunk,),
        out_shape=jax.ShapeDtypeStruct((total_ids, rows * BS, LANES), jnp.bfloat16),
        in_specs=[smem_spec()] * 3 + [whole((rows, ka, BS, BS)), whole((panel_count, BS, kp * BS))],
        out_specs=pl.BlockSpec((chunk, rows * BS, LANES), lambda k: (k, 0, 0)),
        scratch_shapes=[
            pltpu.VMEM((panel_count, 3 * BS, kp * BS), jnp.bfloat16),
            pltpu.VMEM((total_ids, rows, BS, LANES), jnp.float32),
        ],
        compiler_params=pltpu.CompilerParams(vmem_limit_bytes=63000 * 1024),
        name="block_products",
    )(operator_cols, halo_count, meta, blocks, table)

    summed = pl.pallas_call(
        functools.partial(exchange_kernel, n_grp, n_dom, rows, hs, kp, kc, cap, row_at),
        out_shape=f32(owned, BS, kc * BS),
        in_specs=[smem_spec()] * 3 + [vmem_spec()] * 2,
        out_specs=vmem_spec(),
        scratch_shapes=[
            pltpu.VMEM((used, BS, kc * BS), jnp.float32),
            pltpu.VMEM((n_dom - 1, BS, kc * BS), jnp.float32),
            sem((n_dom - 1,)), sem((n_dom - 1,)),
        ],
        compiler_params=pltpu.CompilerParams(
            collective_id=1, has_side_effects=True, vmem_limit_bytes=63000 * 1024
        ),
        name="sum_rows",
    )(prolong_slot, slot_owner_row, meta, packed, prolong)
    return summed.reshape(owned, BS, kc, BS).transpose(0, 2, 1, 3).reshape(owned, kc, BS * BS)


def solution(mesh):
    blocks = P(("grp", "dom"), None, None)
    lists = P(("grp", "dom"), None)
    return jax.shard_map(
        per_device,
        mesh=mesh,
        in_specs=(blocks, lists, P(("grp", "dom")), blocks, lists, lists, lists, lists, lists),
        out_specs=blocks,
        check_vma=False,
    )
```

```python
import functools

import jax
import jax.numpy as jnp
from jax import lax
from jax.experimental import pallas as pl
from jax.experimental.pallas import tpu as pltpu
from jax.sharding import PartitionSpec as P

BS = 64
KG = 12
KH = 4
LANES = 128


def any_spec():
    return pl.BlockSpec(memory_space=pl.ANY)


def vmem_spec():
    return pl.BlockSpec(memory_space=pltpu.VMEM)


def smem_spec():
    return pl.BlockSpec(memory_space=pltpu.SMEM)


def gather_kernel(
    n_grp, n_dom, rows, hs,
    halo, panels, outgoing, dom_meta, grp_meta, operator,
    table, meta, stacked,
    blocks, own_sem, line_send, line_recv, dom_send, dom_recv, meta_send, meta_recv,
):
    g = lax.axis_index("grp")
    me = lax.axis_index("dom")
    far_base = n_grp * rows
    barrier = pltpu.get_barrier_semaphore()
    for k in range(1, n_grp):
        pl.semaphore_signal(barrier, inc=1, device_id={"grp": lax.rem(g + k, n_grp)})
    for k in range(1, n_dom):
        pl.semaphore_signal(barrier, inc=1, device_id={"dom": lax.rem(me + k, n_dom)})
    pl.semaphore_wait(barrier, n_grp + n_dom - 2)

    def line_copy(direction, step, r, src, origin):
        target = g + 1 if direction == 0 else g - 1
        return pltpu.make_async_remote_copy(
            src_ref=src,
            dst_ref=table.at[origin * rows + r],
            send_sem=line_send.at[direction, step, r],
            recv_sem=line_recv.at[direction, step, r],
            device_id={"grp": target},
        )

    can_send = (g < n_grp - 1, g > 0)
    for r in range(rows):
        for direction in range(2):
            @pl.when(can_send[direction])
            def _():
                line_copy(direction, 0, r, panels.at[r], g).start()

    def meta_copy(k, over_dom):
        if over_dom:
            target = lax.rem(me + k, n_dom)
            return pltpu.make_async_remote_copy(
                src_ref=dom_meta.at[target], dst_ref=meta.at[n_grp + me],
                send_sem=meta_send.at[n_grp + k], recv_sem=meta_recv.at[n_grp + k],
                device_id={"dom": target},
            )
        return pltpu.make_async_remote_copy(
            src_ref=grp_meta, dst_ref=meta.at[g],
            send_sem=meta_send.at[k], recv_sem=meta_recv.at[k],
            device_id={"grp": lax.rem(g + k, n_grp)},
        )

    def dom_copy(k):
        target = lax.rem(me + k, n_dom)
        return pltpu.make_async_remote_copy(
            src_ref=outgoing.at[pl.ds(target * hs, hs)],
            dst_ref=table.at[pl.ds(far_base + me * hs, hs)],
            send_sem=dom_send.at[k], recv_sem=dom_recv.at[k],
            device_id={"dom": target},
        )

    for k in range(1, n_grp):
        meta_copy(k, False).start()
    for k in range(1, n_dom):
        dom_copy(k).start()
        meta_copy(k, True).start()
    own = (
        pltpu.make_async_copy(panels, table.at[pl.ds(g * rows, rows)], own_sem.at[0]),
        pltpu.make_async_copy(outgoing.at[pl.ds(me * hs, hs)], table.at[pl.ds(far_base + me * hs, hs)], own_sem.at[1]),
        pltpu.make_async_copy(grp_meta, meta.at[g], own_sem.at[2]),
        pltpu.make_async_copy(dom_meta.at[me], meta.at[n_grp + me], own_sem.at[3]),
    )
    for copy in own:
        copy.start()

    def relay_row(i, carry):
        row = operator[i]
        for a in range(BS):
            blocks[i, :, a, :] = row[:, a * BS:(a + 1) * BS]
        return carry

    def split_row(i, carry):
        for m in range(blocks.shape[1]):
            block = blocks[i, m]
            if m >= KG:
                block = jnp.where(m - KG < halo[i], block, 0.0)
            high = block.astype(jnp.bfloat16).astype(jnp.float32)
            stacked[i, m] = jnp.concatenate([high, high, block - high], axis=1).astype(jnp.bfloat16)
        return carry

    lax.fori_loop(0, rows, relay_row, 0)
    lax.fori_loop(0, rows, split_row, 0)

    def origin_of(direction, step):
        return g - 1 - step if direction == 0 else g + 1 + step

    for step in range(n_grp - 1):
        for r in range(rows):
            for direction in range(2):
                origin = origin_of(direction, step)
                exists = (origin >= 0) & (origin < n_grp)

                @pl.when(exists)
                def _():
                    src = table.at[origin * rows + r]
                    line_copy(direction, step, r, src, origin).wait_recv()

                if step < n_grp - 2:
                    @pl.when(exists & can_send[direction])
                    def _():
                        src = table.at[origin * rows + r]
                        line_copy(direction, step + 1, r, src, origin).start()

    for copy in own:
        copy.wait()
    for k in range(1, n_grp):
        meta_copy(k, False).wait()
    for k in range(1, n_dom):
        dom_copy(k).wait()
        meta_copy(k, True).wait()
    for step in range(n_grp - 1):
        for r in range(rows):
            for direction in range(2):
                origin = g - step if direction == 0 else g + step
                exists = (origin >= 0) & (origin < n_grp)

                @pl.when(exists & can_send[direction])
                def _():
                    line_copy(direction, step, r, panels.at[r], origin).wait_send()


def split_pair(x):
    high = x.astype(jnp.bfloat16)
    low = (x - high.astype(jnp.float32)).astype(jnp.bfloat16)
    return high, low


def product_kernel(
    n_grp, n_dom, rows, hs, ka, kp,
    cols, meta,
    operator, table,
    out,
    split_table, total,
):
    k = pl.program_id(0)
    panel_count = table.shape[0]
    near_count = n_grp * rows
    lane = lax.broadcasted_iota(jnp.int32, (BS, LANES), 1) < BS

    @pl.when(k == 0)
    def _():
        def clear(e, carry):
            total[e] = jnp.zeros(total.shape[1:], jnp.float32)
            return carry

        lax.fori_loop(0, total.shape[0], clear, 0)

        def split(p, carry):
            high, low = split_pair(table[p])
            split_table[p, 0:BS] = high
            split_table[p, BS:2 * BS] = low
            split_table[p, 2 * BS:3 * BS] = high
            return carry

        lax.fori_loop(0, panel_count, split, 0)

        def pairs(m, carry):
            near = m < KG
            products = []
            places = []
            for i in range(rows):
                col = cols[i, m]
                panel = jnp.where(near, col, near_count + col)
                meta_row = jnp.where(near, col // rows, n_grp + col // hs)
                meta_lane = jnp.where(near, (col % rows) * kp, (col % hs) * kp)
                products.append(
                    jnp.dot(operator[i, m], split_table[panel], preferred_element_type=jnp.float32)
                )
                places.append((meta_row, meta_lane))
            for i in range(rows):
                for q in range(0, kp, 2):
                    piece = products[i][:, q * BS:(q + 2) * BS]
                    turned = pltpu.roll(piece, BS, 1)
                    first = meta[places[i][0], 0, places[i][1] + q]
                    second = meta[places[i][0], 0, places[i][1] + q + 1]
                    total[first, i] += jnp.where(lane, piece, turned)
                    total[second, i] += jnp.where(lane, turned, piece)
            return carry

        lax.fori_loop(0, ka, pairs, 0)

    chunk = out.shape[0]
    half = lax.broadcasted_iota(jnp.int32, (rows * BS, LANES), 1) < BS

    def fold(t, carry):
        value = total[k * chunk + t].reshape(rows * BS, LANES)
        high = value.astype(jnp.bfloat16).astype(jnp.float32)
        out[t] = jnp.where(half, high, value - high).astype(jnp.bfloat16)
        return carry

    lax.fori_loop(0, chunk, fold, 0, unroll=4)


def exchange_kernel(
    n_grp, n_dom, rows, hs, kp, kc, cap, row_at,
    slots, owner, meta, packed, prolong,
    out,
    partial, arrived, send_sem, recv_sem,
):
    me = lax.axis_index("dom")
    barrier = pltpu.get_barrier_semaphore()
    for k in range(1, n_dom):
        pl.semaphore_signal(barrier, inc=1, device_id={"dom": lax.rem(me + k, n_dom)})
    pl.semaphore_wait(barrier, n_dom - 1)
    lane = lax.broadcasted_iota(jnp.int32, (BS, LANES), 1) < BS

    def slot_rows(owner_dom, slot, at):
        owner_row = owner[0, slot]
        pattern_at = hs * kp + owner_row * kc
        left = []
        for i in range(rows):
            place = jnp.int32(kp)
            for j in range(kp):
                place = jnp.where(slots[i, j] == slot, j, place)
            block = prolong[i, jnp.minimum(place, kp - 1)]
            left.append(jnp.where(place < kp, block, 0.0).T)
        left_high, left_low = split_pair(jnp.concatenate(left, axis=1))
        both = jnp.concatenate([left_high, left_low], axis=0)
        for c in range(0, kc, 2):
            right = jnp.concatenate(
                [packed[meta[n_grp + owner_dom, 0, pattern_at + c + h]] for h in range(2)], axis=1
            )
            stacked = jnp.dot(both, right, preferred_element_type=jnp.float32)
            both_sum = stacked[:BS] + stacked[BS:]
            folded = []
            for h in range(2):
                piece = both_sum[:, h * LANES:(h + 1) * LANES]
                folded.append(piece + pltpu.roll(piece, BS, 1))
            partial[at, :, c * BS:(c + 2) * BS] = jnp.where(lane, folded[0], folded[1])

    assert n_dom & (n_dom - 1) == 0

    def partner(k):
        other = 0
        bit = 1
        while bit < n_dom:
            other += lax.rem(me // bit + k // bit, 2) * bit
            bit *= 2
        return other

    def copy_of(k):
        target = partner(k)
        return pltpu.make_async_remote_copy(
            src_ref=partial.at[k], dst_ref=arrived.at[k - 1],
            send_sem=send_sem.at[k - 1], recv_sem=recv_sem.at[k - 1],
            device_id={"dom": target},
        )

    def far_slot(step, carry):
        k = n_dom - step
        target = partner(k)
        slot_rows(target, target * cap, k)

        @pl.when(step > 1)
        def _():
            copy_of(k + 1).start()

        return carry

    lax.fori_loop(1, n_dom, far_slot, 0)
    slot_rows(me, me * cap, 0)
    copy_of(1).start()
    owned = out.shape[0]
    for r in range(owned):
        out[r] = partial[0] * (owner[0, me * cap] == r).astype(jnp.float32)
    for t in range(1, cap):
        slot_rows(me, me * cap + t, n_dom + t - 1)
        for r in range(owned):
            out[r] += partial[n_dom + t - 1] * (owner[0, me * cap + t] == r).astype(jnp.float32)
    for k in range(n_dom - 1, 0, -1):
        copy_of(k).wait_recv()
        source = partner(k)
        row = meta[n_grp + source, 0, row_at]
        for r in range(owned):
            out[r] += arrived[k - 1] * (row == r).astype(jnp.float32)
    for k in range(1, n_dom):
        copy_of(k).wait_send()


def prepare_kernel(
    n_dom, rows, hs, kp, kc, cap,
    picked, owner, prolong_raw, prolong_cols, pattern,
    panels, outgoing, prolong, dom_meta, grp_meta,
):
    owned = pattern.shape[0]
    for i in range(rows):
        raw = prolong_raw[i]
        for a in range(BS):
            prolong[i, :, a, :] = raw[:, a * BS:(a + 1) * BS]
        for q in range(0, kp, 2):
            panels[i, :, q * BS:(q + 2) * BS] = jnp.concatenate([prolong[i, q], prolong[i, q + 1]], axis=1)
    grp_meta[...] = jnp.zeros(grp_meta.shape, jnp.int32)
    dom_meta[...] = jnp.zeros(dom_meta.shape, jnp.int32)
    for i in range(rows):
        grp_meta[:, i * kp:(i + 1) * kp] = prolong_cols[i:i + 1, :]
    row_at = hs * kp + owned * kc

    def for_dom(d, carry):
        for h in range(hs):
            row = picked[0, d * hs + h]
            outgoing[d * hs + h] = panels[row]
            dom_meta[d, :, h * kp:(h + 1) * kp] = prolong_cols[pl.ds(row, 1), :]
        for r in range(owned):
            at = hs * kp + r * kc
            dom_meta[d, :, at:at + kc] = pattern[r:r + 1, :]
        dom_meta[d, :, row_at:row_at + 1] = jnp.full((1, 1), owner[0, d * cap], jnp.int32)
        return carry

    lax.fori_loop(0, n_dom, for_dom, 0)


def per_device(
    operator_blocks, operator_cols, halo_count, prolong_blocks, prolong_cols,
    prolong_slot, send_lists, slot_owner_row, coarse_pattern,
):
    n_grp = lax.axis_size("grp")
    n_dom = lax.axis_size("dom")
    rows, ka = operator_cols.shape
    kp = prolong_cols.shape[1]
    owned, kc = coarse_pattern.shape
    hs = send_lists.shape[1] // n_dom
    cap = slot_owner_row.shape[1] // n_dom
    total_ids = owned * n_grp * n_dom
    used = n_dom + cap - 1
    panel_count = n_grp * rows + n_dom * hs
    row_at = hs * kp + owned * kc
    f32 = lambda *shape: jax.ShapeDtypeStruct(shape, jnp.float32)
    i32 = lambda *shape: jax.ShapeDtypeStruct(shape, jnp.int32)

    panels, outgoing, prolong, dom_meta, grp_meta = pl.pallas_call(
        functools.partial(prepare_kernel, n_dom, rows, hs, kp, kc, cap),
        out_shape=(
            f32(rows, BS, kp * BS), f32(n_dom * hs, BS, kp * BS), f32(rows, kp, BS, BS),
            i32(n_dom, 1, LANES), i32(1, LANES),
        ),
        in_specs=[smem_spec()] * 2 + [vmem_spec()] * 3,
        out_specs=(vmem_spec(),) * 5,
        name="prepare",
    )(send_lists, slot_owner_row, prolong_blocks, prolong_cols, coarse_pattern)

    sem = pltpu.SemaphoreType.DMA
    table, meta, stacked = pl.pallas_call(
        functools.partial(gather_kernel, n_grp, n_dom, rows, hs),
        out_shape=(
            f32(panel_count, BS, kp * BS), i32(n_grp + n_dom, 1, LANES),
            jax.ShapeDtypeStruct((rows, ka, BS, 3 * BS), jnp.bfloat16),
        ),
        in_specs=[smem_spec()] + [vmem_spec()] * 5,
        out_specs=(any_spec(), any_spec(), vmem_spec()),
        scratch_shapes=[
            pltpu.VMEM((rows, ka, BS, BS), jnp.float32),
            sem((4,)), sem((2, n_grp - 1, rows)), sem((2, n_grp - 1, rows)),
            sem((n_dom,)), sem((n_dom,)), sem((n_grp + n_dom,)), sem((n_grp + n_dom,)),
        ],
        compiler_params=pltpu.CompilerParams(collective_id=0, has_side_effects=True),
        name="gather_rows",
    )(halo_count, panels, outgoing, dom_meta, grp_meta, operator_blocks)

    whole = lambda shape: pl.BlockSpec(shape, lambda k: (0,) * len(shape), pipeline_mode=pl.Buffered(1))
    chunk = 8
    packed = pl.pallas_call(
        functools.partial(product_kernel, n_grp, n_dom, rows, hs, ka, kp),
        grid=(total_ids // chunk,),
        out_shape=jax.ShapeDtypeStruct((total_ids, rows * BS, LANES), jnp.bfloat16),
        in_specs=[smem_spec()] * 2 + [whole((rows, ka, BS, 3 * BS)), whole((panel_count, BS, kp * BS))],
        out_specs=pl.BlockSpec((chunk, rows * BS, LANES), lambda k: (k, 0, 0)),
        scratch_shapes=[
            pltpu.VMEM((panel_count, 3 * BS, kp * BS), jnp.bfloat16),
            pltpu.VMEM((total_ids, rows, BS, LANES), jnp.float32),
        ],
        compiler_params=pltpu.CompilerParams(vmem_limit_bytes=63000 * 1024),
        name="block_products",
    )(operator_cols, meta, stacked, table)

    summed = pl.pallas_call(
        functools.partial(exchange_kernel, n_grp, n_dom, rows, hs, kp, kc, cap, row_at),
        out_shape=f32(owned, BS, kc * BS),
        in_specs=[smem_spec()] * 3 + [vmem_spec()] * 2,
        out_specs=vmem_spec(),
        scratch_shapes=[
            pltpu.VMEM((used, BS, kc * BS), jnp.float32),
            pltpu.VMEM((n_dom - 1, BS, kc * BS), jnp.float32),
            sem((n_dom - 1,)), sem((n_dom - 1,)),
        ],
        compiler_params=pltpu.CompilerParams(
            collective_id=1, has_side_effects=True, vmem_limit_bytes=63000 * 1024
        ),
        name="sum_rows",
    )(prolong_slot, slot_owner_row, meta, packed, prolong)
    return summed.reshape(owned, BS, kc, BS).transpose(0, 2, 1, 3).reshape(owned, kc, BS * BS)


def solution(mesh):
    blocks = P(("grp", "dom"), None, None)
    lists = P(("grp", "dom"), None)
    return jax.shard_map(
        per_device,
        mesh=mesh,
        in_specs=(blocks, lists, P(("grp", "dom")), blocks, lists, lists, lists, lists, lists),
        out_specs=blocks,
        check_vma=False,
    )
```

```python
import functools

import jax
import jax.numpy as jnp
from jax import lax
from jax.experimental import pallas as pl
from jax.experimental.pallas import tpu as pltpu
from jax.sharding import PartitionSpec as P

BS = 64
KG = 12
KH = 4
LANES = 128


def any_spec():
    return pl.BlockSpec(memory_space=pl.ANY)


def vmem_spec():
    return pl.BlockSpec(memory_space=pltpu.VMEM)


def smem_spec():
    return pl.BlockSpec(memory_space=pltpu.SMEM)


def prepare_rows(
    n_dom, rows, hs, kp, kc, cap,
    picked, owner, prolong_raw, prolong_cols, pattern,
    panels, outgoing, prolong, dom_meta, grp_meta,
):
    owned = pattern.shape[0]
    for i in range(rows):
        raw = prolong_raw[i]
        for a in range(BS):
            prolong[i, :, a, :] = raw[:, a * BS:(a + 1) * BS]
        for q in range(0, kp, 2):
            panels[i, :, q * BS:(q + 2) * BS] = jnp.concatenate([prolong[i, q], prolong[i, q + 1]], axis=1)
    grp_meta[...] = jnp.zeros(grp_meta.shape, jnp.int32)
    dom_meta[...] = jnp.zeros(dom_meta.shape, jnp.int32)
    for i in range(rows):
        grp_meta[:, i * kp:(i + 1) * kp] = prolong_cols[i:i + 1, :]
    row_at = hs * kp + owned * kc

    def for_dom(d, carry):
        for h in range(hs):
            row = picked[0, d * hs + h]
            outgoing[d * hs + h] = panels[row]
            dom_meta[d, :, h * kp:(h + 1) * kp] = prolong_cols[pl.ds(row, 1), :]
        for r in range(owned):
            at = hs * kp + r * kc
            dom_meta[d, :, at:at + kc] = pattern[r:r + 1, :]
        dom_meta[d, :, row_at:row_at + 1] = jnp.full((1, 1), owner[0, d * cap], jnp.int32)
        return carry

    lax.fori_loop(0, n_dom, for_dom, 0)


def gather_kernel(
    n_grp, n_dom, rows, hs, kp, kc, cap,
    halo, picked, owner, prolong_raw, prolong_cols, pattern, operator,
    table, meta, stacked, prolong,
    panels, outgoing, dom_meta, grp_meta, blocks, own_sem, line_send, line_recv, dom_send, dom_recv, meta_send, meta_recv,
):
    g = lax.axis_index("grp")
    me = lax.axis_index("dom")
    far_base = n_grp * rows
    barrier = pltpu.get_barrier_semaphore()
    for k in range(1, n_grp):
        pl.semaphore_signal(barrier, inc=1, device_id={"grp": lax.rem(g + k, n_grp)})
    for k in range(1, n_dom):
        pl.semaphore_signal(barrier, inc=1, device_id={"dom": lax.rem(me + k, n_dom)})
    prepare_rows(
        n_dom, rows, hs, kp, kc, cap,
        picked, owner, prolong_raw, prolong_cols, pattern,
        panels, outgoing, prolong, dom_meta, grp_meta,
    )
    pl.semaphore_wait(barrier, n_grp + n_dom - 2)

    def line_copy(direction, step, r, src, origin):
        target = g + 1 if direction == 0 else g - 1
        return pltpu.make_async_remote_copy(
            src_ref=src,
            dst_ref=table.at[origin * rows + r],
            send_sem=line_send.at[direction, step, r],
            recv_sem=line_recv.at[direction, step, r],
            device_id={"grp": target},
        )

    can_send = (g < n_grp - 1, g > 0)
    for r in range(rows):
        for direction in range(2):
            @pl.when(can_send[direction])
            def _():
                line_copy(direction, 0, r, panels.at[r], g).start()

    def meta_copy(k, over_dom):
        if over_dom:
            target = lax.rem(me + k, n_dom)
            return pltpu.make_async_remote_copy(
                src_ref=dom_meta.at[target], dst_ref=meta.at[n_grp + me],
                send_sem=meta_send.at[n_grp + k], recv_sem=meta_recv.at[n_grp + k],
                device_id={"dom": target},
            )
        return pltpu.make_async_remote_copy(
            src_ref=grp_meta, dst_ref=meta.at[g],
            send_sem=meta_send.at[k], recv_sem=meta_recv.at[k],
            device_id={"grp": lax.rem(g + k, n_grp)},
        )

    def dom_copy(k):
        target = lax.rem(me + k, n_dom)
        return pltpu.make_async_remote_copy(
            src_ref=outgoing.at[pl.ds(target * hs, hs)],
            dst_ref=table.at[pl.ds(far_base + me * hs, hs)],
            send_sem=dom_send.at[k], recv_sem=dom_recv.at[k],
            device_id={"dom": target},
        )

    for k in range(1, n_grp):
        meta_copy(k, False).start()
    for k in range(1, n_dom):
        dom_copy(k).start()
        meta_copy(k, True).start()
    own = (
        pltpu.make_async_copy(panels, table.at[pl.ds(g * rows, rows)], own_sem.at[0]),
        pltpu.make_async_copy(outgoing.at[pl.ds(me * hs, hs)], table.at[pl.ds(far_base + me * hs, hs)], own_sem.at[1]),
        pltpu.make_async_copy(grp_meta, meta.at[g], own_sem.at[2]),
        pltpu.make_async_copy(dom_meta.at[me], meta.at[n_grp + me], own_sem.at[3]),
    )
    for copy in own:
        copy.start()

    def relay_row(i, carry):
        row = operator[i]
        for a in range(BS):
            blocks[i, :, a, :] = row[:, a * BS:(a + 1) * BS]
        return carry

    def split_row(i, carry):
        for m in range(blocks.shape[1]):
            block = blocks[i, m]
            if m >= KG:
                block = jnp.where(m - KG < halo[i], block, 0.0)
            high = block.astype(jnp.bfloat16).astype(jnp.float32)
            stacked[i, m] = jnp.concatenate([high, high, block - high], axis=1).astype(jnp.bfloat16)
        return carry

    lax.fori_loop(0, rows, relay_row, 0)
    lax.fori_loop(0, rows, split_row, 0)

    def origin_of(direction, step):
        return g - 1 - step if direction == 0 else g + 1 + step

    for step in range(n_grp - 1):
        for r in range(rows):
            for direction in range(2):
                origin = origin_of(direction, step)
                exists = (origin >= 0) & (origin < n_grp)

                @pl.when(exists)
                def _():
                    src = table.at[origin * rows + r]
                    line_copy(direction, step, r, src, origin).wait_recv()

                if step < n_grp - 2:
                    @pl.when(exists & can_send[direction])
                    def _():
                        src = table.at[origin * rows + r]
                        line_copy(direction, step + 1, r, src, origin).start()

    for copy in own:
        copy.wait()
    for k in range(1, n_grp):
        meta_copy(k, False).wait()
    for k in range(1, n_dom):
        dom_copy(k).wait()
        meta_copy(k, True).wait()
    for step in range(n_grp - 1):
        for r in range(rows):
            for direction in range(2):
                origin = g - step if direction == 0 else g + step
                exists = (origin >= 0) & (origin < n_grp)

                @pl.when(exists & can_send[direction])
                def _():
                    line_copy(direction, step, r, panels.at[r], origin).wait_send()


def split_pair(x):
    high = x.astype(jnp.bfloat16)
    low = (x - high.astype(jnp.float32)).astype(jnp.bfloat16)
    return high, low


def product_kernel(
    n_grp, n_dom, rows, hs, ka, kp,
    cols, meta,
    operator, table,
    out,
    split_table, total,
):
    k = pl.program_id(0)
    panel_count = table.shape[0]
    near_count = n_grp * rows
    lane = lax.broadcasted_iota(jnp.int32, (BS, LANES), 1) < BS

    @pl.when(k == 0)
    def _():
        def clear(e, carry):
            total[e] = jnp.zeros(total.shape[1:], jnp.float32)
            return carry

        lax.fori_loop(0, total.shape[0], clear, 0)

        def split(p, carry):
            high, low = split_pair(table[p])
            split_table[p, 0:BS] = high
            split_table[p, BS:2 * BS] = low
            split_table[p, 2 * BS:3 * BS] = high
            return carry

        lax.fori_loop(0, panel_count, split, 0)

        def pairs(m, carry):
            near = m < KG
            products = []
            places = []
            for i in range(rows):
                col = cols[i, m]
                panel = jnp.where(near, col, near_count + col)
                meta_row = jnp.where(near, col // rows, n_grp + col // hs)
                meta_lane = jnp.where(near, (col % rows) * kp, (col % hs) * kp)
                products.append(
                    jnp.dot(operator[i, m], split_table[panel], preferred_element_type=jnp.float32)
                )
                places.append((meta_row, meta_lane))
            for i in range(rows):
                for q in range(0, kp, 2):
                    piece = products[i][:, q * BS:(q + 2) * BS]
                    turned = pltpu.roll(piece, BS, 1)
                    first = meta[places[i][0], 0, places[i][1] + q]
                    second = meta[places[i][0], 0, places[i][1] + q + 1]
                    total[first, i] += jnp.where(lane, piece, turned)
                    total[second, i] += jnp.where(lane, turned, piece)
            return carry

        lax.fori_loop(0, ka, pairs, 0)

    chunk = out.shape[0]
    half = lax.broadcasted_iota(jnp.int32, (rows * BS, LANES), 1) < BS

    def fold(t, carry):
        value = total[k * chunk + t].reshape(rows * BS, LANES)
        high = value.astype(jnp.bfloat16).astype(jnp.float32)
        out[t] = jnp.where(half, high, value - high).astype(jnp.bfloat16)
        return carry

    lax.fori_loop(0, chunk, fold, 0, unroll=4)


def exchange_kernel(
    n_grp, n_dom, rows, hs, kp, kc, cap, row_at,
    slots, owner, meta, packed, prolong,
    out,
    partial, arrived, summed, send_sem, recv_sem,
):
    me = lax.axis_index("dom")
    barrier = pltpu.get_barrier_semaphore()
    for k in range(1, n_dom):
        pl.semaphore_signal(barrier, inc=1, device_id={"dom": lax.rem(me + k, n_dom)})
    pl.semaphore_wait(barrier, n_dom - 1)
    lane = lax.broadcasted_iota(jnp.int32, (BS, LANES), 1) < BS

    def slot_rows(owner_dom, slot, at):
        owner_row = owner[0, slot]
        pattern_at = hs * kp + owner_row * kc
        left = []
        for i in range(rows):
            place = jnp.int32(kp)
            for j in range(kp):
                place = jnp.where(slots[i, j] == slot, j, place)
            block = prolong[i, jnp.minimum(place, kp - 1)]
            left.append(jnp.where(place < kp, block, 0.0).T)
        left_high, left_low = split_pair(jnp.concatenate(left, axis=1))
        both = jnp.concatenate([left_high, left_low], axis=0)
        for c in range(0, kc, 2):
            right = jnp.concatenate(
                [packed[meta[n_grp + owner_dom, 0, pattern_at + c + h]] for h in range(2)], axis=1
            )
            stacked = jnp.dot(both, right, preferred_element_type=jnp.float32)
            both_sum = stacked[:BS] + stacked[BS:]
            folded = []
            for h in range(2):
                piece = both_sum[:, h * LANES:(h + 1) * LANES]
                folded.append(piece + pltpu.roll(piece, BS, 1))
            partial[at, :, c * BS:(c + 2) * BS] = jnp.where(lane, folded[0], folded[1])

    assert n_dom & (n_dom - 1) == 0

    def partner(k):
        other = 0
        bit = 1
        while bit < n_dom:
            other += lax.rem(me // bit + k // bit, 2) * bit
            bit *= 2
        return other

    def copy_of(k):
        target = partner(k)
        return pltpu.make_async_remote_copy(
            src_ref=partial.at[k], dst_ref=arrived.at[k - 1],
            send_sem=send_sem.at[k - 1], recv_sem=recv_sem.at[k - 1],
            device_id={"dom": target},
        )

    def far_slot(step, carry):
        k = n_dom - step
        target = partner(k)
        slot_rows(target, target * cap, k)

        @pl.when(step > 1)
        def _():
            copy_of(k + 1).start()

        return carry

    lax.fori_loop(1, n_dom, far_slot, 0)
    slot_rows(me, me * cap, 0)
    copy_of(1).start()
    owned = out.shape[0]
    for r in range(owned):
        summed[r] = partial[0] * (owner[0, me * cap] == r).astype(jnp.float32)
    for t in range(1, cap):
        slot_rows(me, me * cap + t, n_dom + t - 1)
        for r in range(owned):
            summed[r] += partial[n_dom + t - 1] * (owner[0, me * cap + t] == r).astype(jnp.float32)
    for k in range(n_dom - 1, 0, -1):
        copy_of(k).wait_recv()
        source = partner(k)
        row = meta[n_grp + source, 0, row_at]
        for r in range(owned):
            summed[r] += arrived[k - 1] * (row == r).astype(jnp.float32)
    for r in range(owned):
        for c in range(kc):
            out[r, c] = summed[r, :, c * BS:(c + 1) * BS]
    for k in range(1, n_dom):
        copy_of(k).wait_send()


def per_device(
    operator_blocks, operator_cols, halo_count, prolong_blocks, prolong_cols,
    prolong_slot, send_lists, slot_owner_row, coarse_pattern,
):
    n_grp = lax.axis_size("grp")
    n_dom = lax.axis_size("dom")
    rows, ka = operator_cols.shape
    kp = prolong_cols.shape[1]
    owned, kc = coarse_pattern.shape
    hs = send_lists.shape[1] // n_dom
    cap = slot_owner_row.shape[1] // n_dom
    total_ids = owned * n_grp * n_dom
    used = n_dom + cap - 1
    panel_count = n_grp * rows + n_dom * hs
    row_at = hs * kp + owned * kc
    f32 = lambda *shape: jax.ShapeDtypeStruct(shape, jnp.float32)
    i32 = lambda *shape: jax.ShapeDtypeStruct(shape, jnp.int32)

    sem = pltpu.SemaphoreType.DMA
    table, meta, stacked, prolong = pl.pallas_call(
        functools.partial(gather_kernel, n_grp, n_dom, rows, hs, kp, kc, cap),
        out_shape=(
            f32(panel_count, BS, kp * BS), i32(n_grp + n_dom, 1, LANES),
            jax.ShapeDtypeStruct((rows, ka, BS, 3 * BS), jnp.bfloat16), f32(rows, kp, BS, BS),
        ),
        in_specs=[smem_spec()] * 3 + [vmem_spec()] * 4,
        out_specs=(any_spec(), any_spec(), vmem_spec(), vmem_spec()),
        scratch_shapes=[
            pltpu.VMEM((rows, BS, kp * BS), jnp.float32),
            pltpu.VMEM((n_dom * hs, BS, kp * BS), jnp.float32),
            pltpu.VMEM((n_dom, 1, LANES), jnp.int32),
            pltpu.VMEM((1, LANES), jnp.int32),
            pltpu.VMEM((rows, ka, BS, BS), jnp.float32),
            sem((4,)), sem((2, n_grp - 1, rows)), sem((2, n_grp - 1, rows)),
            sem((n_dom,)), sem((n_dom,)), sem((n_grp + n_dom,)), sem((n_grp + n_dom,)),
        ],
        compiler_params=pltpu.CompilerParams(collective_id=0, has_side_effects=True),
        name="gather_rows",
    )(
        halo_count, send_lists, slot_owner_row, prolong_blocks, prolong_cols, coarse_pattern, operator_blocks
    )

    whole = lambda shape: pl.BlockSpec(shape, lambda k: (0,) * len(shape), pipeline_mode=pl.Buffered(1))
    chunk = 8
    packed = pl.pallas_call(
        functools.partial(product_kernel, n_grp, n_dom, rows, hs, ka, kp),
        grid=(total_ids // chunk,),
        out_shape=jax.ShapeDtypeStruct((total_ids, rows * BS, LANES), jnp.bfloat16),
        in_specs=[smem_spec()] * 2 + [whole((rows, ka, BS, 3 * BS)), whole((panel_count, BS, kp * BS))],
        out_specs=pl.BlockSpec((chunk, rows * BS, LANES), lambda k: (k, 0, 0)),
        scratch_shapes=[
            pltpu.VMEM((panel_count, 3 * BS, kp * BS), jnp.bfloat16),
            pltpu.VMEM((total_ids, rows, BS, LANES), jnp.float32),
        ],
        compiler_params=pltpu.CompilerParams(vmem_limit_bytes=63000 * 1024),
        name="block_products",
    )(operator_cols, meta, stacked, table)

    summed = pl.pallas_call(
        functools.partial(exchange_kernel, n_grp, n_dom, rows, hs, kp, kc, cap, row_at),
        out_shape=f32(owned, kc, BS, BS),
        in_specs=[smem_spec()] * 3 + [vmem_spec()] * 2,
        out_specs=vmem_spec(),
        scratch_shapes=[
            pltpu.VMEM((used, BS, kc * BS), jnp.float32),
            pltpu.VMEM((n_dom - 1, BS, kc * BS), jnp.float32),
            pltpu.VMEM((owned, BS, kc * BS), jnp.float32),
            sem((n_dom - 1,)), sem((n_dom - 1,)),
        ],
        compiler_params=pltpu.CompilerParams(
            collective_id=1, has_side_effects=True, vmem_limit_bytes=63000 * 1024
        ),
        name="sum_rows",
    )(prolong_slot, slot_owner_row, meta, packed, prolong)
    return summed.reshape(owned, kc, BS * BS)


def solution(mesh):
    blocks = P(("grp", "dom"), None, None)
    lists = P(("grp", "dom"), None)
    return jax.shard_map(
        per_device,
        mesh=mesh,
        in_specs=(blocks, lists, P(("grp", "dom")), blocks, lists, lists, lists, lists, lists),
        out_specs=blocks,
        check_vma=False,
    )
```

```python
import functools

import jax
import jax.numpy as jnp
from jax import lax
from jax.experimental import pallas as pl
from jax.experimental.pallas import tpu as pltpu
from jax.sharding import PartitionSpec as P

BS = 64
KG = 12
KH = 4
LANES = 128


def any_spec():
    return pl.BlockSpec(memory_space=pl.ANY)


def vmem_spec():
    return pl.BlockSpec(memory_space=pltpu.VMEM)


def smem_spec():
    return pl.BlockSpec(memory_space=pltpu.SMEM)


def prepare_rows(
    n_dom, rows, hs, kp, kc, cap,
    picked, owner, prolong_raw, prolong_cols, pattern,
    panels, outgoing, prolong, dom_meta, grp_meta,
):
    owned = pattern.shape[0]
    for i in range(rows):
        raw = prolong_raw[i]
        for a in range(BS):
            prolong[i, :, a, :] = raw[:, a * BS:(a + 1) * BS]
        for q in range(0, kp, 2):
            panels[i, :, q * BS:(q + 2) * BS] = jnp.concatenate([prolong[i, q], prolong[i, q + 1]], axis=1)
    grp_meta[...] = jnp.zeros(grp_meta.shape, jnp.int32)
    dom_meta[...] = jnp.zeros(dom_meta.shape, jnp.int32)
    for i in range(rows):
        grp_meta[:, i * kp:(i + 1) * kp] = prolong_cols[i:i + 1, :]
    row_at = hs * kp + owned * kc

    def for_dom(d, carry):
        for h in range(hs):
            row = picked[0, d * hs + h]
            outgoing[d * hs + h] = panels[row]
            dom_meta[d, :, h * kp:(h + 1) * kp] = prolong_cols[pl.ds(row, 1), :]
        for r in range(owned):
            at = hs * kp + r * kc
            dom_meta[d, :, at:at + kc] = pattern[r:r + 1, :]
        dom_meta[d, :, row_at:row_at + 1] = jnp.full((1, 1), owner[0, d * cap], jnp.int32)
        return carry

    lax.fori_loop(0, n_dom, for_dom, 0)


def gather_kernel(
    n_grp, n_dom, rows, hs, kp, kc, cap,
    halo, picked, owner, prolong_raw, prolong_cols, pattern, operator_in,
    table, meta, stacked_out, prolong_out,
    operator, stacked, prolong, bulk_sem,
    panels, outgoing, dom_meta, grp_meta, blocks, own_sem, line_send, line_recv, dom_send, dom_recv, meta_send, meta_recv,
):
    g = lax.axis_index("grp")
    me = lax.axis_index("dom")
    far_base = n_grp * rows
    barrier = pltpu.get_barrier_semaphore()
    for k in range(1, n_grp):
        pl.semaphore_signal(barrier, inc=1, device_id={"grp": lax.rem(g + k, n_grp)})
    for k in range(1, n_dom):
        pl.semaphore_signal(barrier, inc=1, device_id={"dom": lax.rem(me + k, n_dom)})
    operator_copy = pltpu.make_async_copy(operator_in, operator, bulk_sem.at[0])
    operator_copy.start()
    prepare_rows(
        n_dom, rows, hs, kp, kc, cap,
        picked, owner, prolong_raw, prolong_cols, pattern,
        panels, outgoing, prolong, dom_meta, grp_meta,
    )
    pl.semaphore_wait(barrier, n_grp + n_dom - 2)

    def line_copy(direction, step, r, src, origin):
        target = g + 1 if direction == 0 else g - 1
        return pltpu.make_async_remote_copy(
            src_ref=src,
            dst_ref=table.at[origin * rows + r],
            send_sem=line_send.at[direction, step, r],
            recv_sem=line_recv.at[direction, step, r],
            device_id={"grp": target},
        )

    can_send = (g < n_grp - 1, g > 0)
    for r in range(rows):
        for direction in range(2):
            @pl.when(can_send[direction])
            def _():
                line_copy(direction, 0, r, panels.at[r], g).start()

    def meta_copy(k, over_dom):
        if over_dom:
            target = lax.rem(me + k, n_dom)
            return pltpu.make_async_remote_copy(
                src_ref=dom_meta.at[target], dst_ref=meta.at[n_grp + me],
                send_sem=meta_send.at[n_grp + k], recv_sem=meta_recv.at[n_grp + k],
                device_id={"dom": target},
            )
        return pltpu.make_async_remote_copy(
            src_ref=grp_meta, dst_ref=meta.at[g],
            send_sem=meta_send.at[k], recv_sem=meta_recv.at[k],
            device_id={"grp": lax.rem(g + k, n_grp)},
        )

    def dom_copy(k):
        target = lax.rem(me + k, n_dom)
        return pltpu.make_async_remote_copy(
            src_ref=outgoing.at[pl.ds(target * hs, hs)],
            dst_ref=table.at[pl.ds(far_base + me * hs, hs)],
            send_sem=dom_send.at[k], recv_sem=dom_recv.at[k],
            device_id={"dom": target},
        )

    for k in range(1, n_grp):
        meta_copy(k, False).start()
    for k in range(1, n_dom):
        dom_copy(k).start()
        meta_copy(k, True).start()
    own = (
        pltpu.make_async_copy(panels, table.at[pl.ds(g * rows, rows)], own_sem.at[0]),
        pltpu.make_async_copy(outgoing.at[pl.ds(me * hs, hs)], table.at[pl.ds(far_base + me * hs, hs)], own_sem.at[1]),
        pltpu.make_async_copy(grp_meta, meta.at[g], own_sem.at[2]),
        pltpu.make_async_copy(dom_meta.at[me], meta.at[n_grp + me], own_sem.at[3]),
    )
    for copy in own:
        copy.start()

    def relay_row(i, carry):
        row = operator[i]
        for a in range(BS):
            blocks[i, :, a, :] = row[:, a * BS:(a + 1) * BS]
        return carry

    def split_row(i, carry):
        for m in range(blocks.shape[1]):
            block = blocks[i, m]
            if m >= KG:
                block = jnp.where(m - KG < halo[i], block, 0.0)
            high = block.astype(jnp.bfloat16).astype(jnp.float32)
            stacked[i, m] = jnp.concatenate([high, high, block - high], axis=1).astype(jnp.bfloat16)
        return carry

    prolong_copy = pltpu.make_async_copy(prolong, prolong_out, bulk_sem.at[1])
    stacked_copy = pltpu.make_async_copy(stacked, stacked_out, bulk_sem.at[2])
    prolong_copy.start()
    operator_copy.wait()
    lax.fori_loop(0, rows, relay_row, 0)
    lax.fori_loop(0, rows, split_row, 0)
    stacked_copy.start()

    def origin_of(direction, step):
        return g - 1 - step if direction == 0 else g + 1 + step

    for step in range(n_grp - 1):
        for r in range(rows):
            for direction in range(2):
                origin = origin_of(direction, step)
                exists = (origin >= 0) & (origin < n_grp)

                @pl.when(exists)
                def _():
                    src = table.at[origin * rows + r]
                    line_copy(direction, step, r, src, origin).wait_recv()

                if step < n_grp - 2:
                    @pl.when(exists & can_send[direction])
                    def _():
                        src = table.at[origin * rows + r]
                        line_copy(direction, step + 1, r, src, origin).start()

    prolong_copy.wait()
    stacked_copy.wait()
    for copy in own:
        copy.wait()
    for k in range(1, n_grp):
        meta_copy(k, False).wait()
    for k in range(1, n_dom):
        dom_copy(k).wait()
        meta_copy(k, True).wait()
    for step in range(n_grp - 1):
        for r in range(rows):
            for direction in range(2):
                origin = g - step if direction == 0 else g + step
                exists = (origin >= 0) & (origin < n_grp)

                @pl.when(exists & can_send[direction])
                def _():
                    line_copy(direction, step, r, panels.at[r], origin).wait_send()


def split_pair(x):
    high = x.astype(jnp.bfloat16)
    low = (x - high.astype(jnp.float32)).astype(jnp.bfloat16)
    return high, low


def product_kernel(
    n_grp, n_dom, rows, hs, ka, kp,
    cols, meta,
    operator_in, table_in,
    out,
    operator, table, split_table, total, load_sem,
):
    k = pl.program_id(0)
    panel_count = table.shape[0]
    near_count = n_grp * rows
    lane = lax.broadcasted_iota(jnp.int32, (BS, LANES), 1) < BS

    @pl.when(k == 0)
    def _():
        table_copy = pltpu.make_async_copy(table_in, table, load_sem.at[0])
        operator_copy = pltpu.make_async_copy(operator_in, operator, load_sem.at[1])
        table_copy.start()
        operator_copy.start()

        def clear(e, carry):
            total[e] = jnp.zeros(total.shape[1:], jnp.float32)
            return carry

        lax.fori_loop(0, total.shape[0], clear, 0)

        def split(p, carry):
            high, low = split_pair(table[p])
            split_table[p, 0:BS] = high
            split_table[p, BS:2 * BS] = low
            split_table[p, 2 * BS:3 * BS] = high
            return carry

        table_copy.wait()
        lax.fori_loop(0, panel_count, split, 0)
        operator_copy.wait()

        def pairs(m, carry):
            near = m < KG
            products = []
            places = []
            for i in range(rows):
                col = cols[i, m]
                panel = jnp.where(near, col, near_count + col)
                meta_row = jnp.where(near, col // rows, n_grp + col // hs)
                meta_lane = jnp.where(near, (col % rows) * kp, (col % hs) * kp)
                products.append(
                    jnp.dot(operator[i, m], split_table[panel], preferred_element_type=jnp.float32)
                )
                places.append((meta_row, meta_lane))
            for i in range(rows):
                for q in range(0, kp, 2):
                    piece = products[i][:, q * BS:(q + 2) * BS]
                    turned = pltpu.roll(piece, BS, 1)
                    first = meta[places[i][0], 0, places[i][1] + q]
                    second = meta[places[i][0], 0, places[i][1] + q + 1]
                    total[first, i] += jnp.where(lane, piece, turned)
                    total[second, i] += jnp.where(lane, turned, piece)
            return carry

        lax.fori_loop(0, ka, pairs, 0)

    chunk = out.shape[0]
    half = lax.broadcasted_iota(jnp.int32, (rows * BS, LANES), 1) < BS

    def fold(t, carry):
        value = total[k * chunk + t].reshape(rows * BS, LANES)
        high = value.astype(jnp.bfloat16).astype(jnp.float32)
        out[t] = jnp.where(half, high, value - high).astype(jnp.bfloat16)
        return carry

    lax.fori_loop(0, chunk, fold, 0, unroll=4)


def exchange_kernel(
    n_grp, n_dom, rows, hs, kp, kc, cap, row_at,
    slots, owner, meta, packed_in, prolong_in,
    out,
    packed, prolong, load_sem, partial, arrived, summed, send_sem, recv_sem,
):
    me = lax.axis_index("dom")
    loads = (
        pltpu.make_async_copy(packed_in, packed, load_sem.at[0]),
        pltpu.make_async_copy(prolong_in, prolong, load_sem.at[1]),
    )
    for load in loads:
        load.start()
    barrier = pltpu.get_barrier_semaphore()
    for k in range(1, n_dom):
        pl.semaphore_signal(barrier, inc=1, device_id={"dom": lax.rem(me + k, n_dom)})
    pl.semaphore_wait(barrier, n_dom - 1)
    for load in loads:
        load.wait()
    lane = lax.broadcasted_iota(jnp.int32, (BS, LANES), 1) < BS

    def slot_rows(owner_dom, slot, at):
        owner_row = owner[0, slot]
        pattern_at = hs * kp + owner_row * kc
        left = []
        for i in range(rows):
            place = jnp.int32(kp)
            for j in range(kp):
                place = jnp.where(slots[i, j] == slot, j, place)
            block = prolong[i, jnp.minimum(place, kp - 1)]
            left.append(jnp.where(place < kp, block, 0.0).T)
        left_high, left_low = split_pair(jnp.concatenate(left, axis=1))
        both = jnp.concatenate([left_high, left_low], axis=0)
        for c in range(0, kc, 2):
            right = jnp.concatenate(
                [packed[meta[n_grp + owner_dom, 0, pattern_at + c + h]] for h in range(2)], axis=1
            )
            stacked = jnp.dot(both, right, preferred_element_type=jnp.float32)
            both_sum = stacked[:BS] + stacked[BS:]
            folded = []
            for h in range(2):
                piece = both_sum[:, h * LANES:(h + 1) * LANES]
                folded.append(piece + pltpu.roll(piece, BS, 1))
            partial[at, :, c * BS:(c + 2) * BS] = jnp.where(lane, folded[0], folded[1])

    assert n_dom & (n_dom - 1) == 0

    def partner(k):
        other = 0
        bit = 1
        while bit < n_dom:
            other += lax.rem(me // bit + k // bit, 2) * bit
            bit *= 2
        return other

    def copy_of(k):
        target = partner(k)
        return pltpu.make_async_remote_copy(
            src_ref=partial.at[k], dst_ref=arrived.at[k - 1],
            send_sem=send_sem.at[k - 1], recv_sem=recv_sem.at[k - 1],
            device_id={"dom": target},
        )

    def far_slot(step, carry):
        k = n_dom - step
        target = partner(k)
        slot_rows(target, target * cap, k)

        @pl.when(step > 1)
        def _():
            copy_of(k + 1).start()

        return carry

    lax.fori_loop(1, n_dom, far_slot, 0)
    slot_rows(me, me * cap, 0)
    copy_of(1).start()
    owned = out.shape[0]
    for r in range(owned):
        summed[r] = partial[0] * (owner[0, me * cap] == r).astype(jnp.float32)
    for t in range(1, cap):
        slot_rows(me, me * cap + t, n_dom + t - 1)
        for r in range(owned):
            summed[r] += partial[n_dom + t - 1] * (owner[0, me * cap + t] == r).astype(jnp.float32)
    for k in range(n_dom - 1, 0, -1):
        copy_of(k).wait_recv()
        source = partner(k)
        row = meta[n_grp + source, 0, row_at]
        for r in range(owned):
            summed[r] += arrived[k - 1] * (row == r).astype(jnp.float32)
    for r in range(owned):
        for c in range(kc):
            out[r, c] = summed[r, :, c * BS:(c + 1) * BS]
    for k in range(1, n_dom):
        copy_of(k).wait_send()


def per_device(
    operator_blocks, operator_cols, halo_count, prolong_blocks, prolong_cols,
    prolong_slot, send_lists, slot_owner_row, coarse_pattern,
):
    n_grp = lax.axis_size("grp")
    n_dom = lax.axis_size("dom")
    rows, ka = operator_cols.shape
    kp = prolong_cols.shape[1]
    owned, kc = coarse_pattern.shape
    hs = send_lists.shape[1] // n_dom
    cap = slot_owner_row.shape[1] // n_dom
    total_ids = owned * n_grp * n_dom
    used = n_dom + cap - 1
    panel_count = n_grp * rows + n_dom * hs
    row_at = hs * kp + owned * kc
    f32 = lambda *shape: jax.ShapeDtypeStruct(shape, jnp.float32)
    i32 = lambda *shape: jax.ShapeDtypeStruct(shape, jnp.int32)

    sem = pltpu.SemaphoreType.DMA
    table, meta, stacked, prolong = pl.pallas_call(
        functools.partial(gather_kernel, n_grp, n_dom, rows, hs, kp, kc, cap),
        out_shape=(
            f32(panel_count, BS, kp * BS), i32(n_grp + n_dom, 1, LANES),
            jax.ShapeDtypeStruct((rows, ka, BS, 3 * BS), jnp.bfloat16), f32(rows, kp, BS, BS),
        ),
        in_specs=[smem_spec()] * 3 + [vmem_spec()] * 3 + [any_spec()],
        out_specs=(any_spec(),) * 4,
        scratch_shapes=[
            pltpu.VMEM((rows, ka, BS * BS), jnp.float32),
            pltpu.VMEM((rows, ka, BS, 3 * BS), jnp.bfloat16),
            pltpu.VMEM((rows, kp, BS, BS), jnp.float32),
            sem((3,)),
            pltpu.VMEM((rows, BS, kp * BS), jnp.float32),
            pltpu.VMEM((n_dom * hs, BS, kp * BS), jnp.float32),
            pltpu.VMEM((n_dom, 1, LANES), jnp.int32),
            pltpu.VMEM((1, LANES), jnp.int32),
            pltpu.VMEM((rows, ka, BS, BS), jnp.float32),
            sem((4,)), sem((2, n_grp - 1, rows)), sem((2, n_grp - 1, rows)),
            sem((n_dom,)), sem((n_dom,)), sem((n_grp + n_dom,)), sem((n_grp + n_dom,)),
        ],
        compiler_params=pltpu.CompilerParams(collective_id=0, has_side_effects=True),
        name="gather_rows",
    )(
        halo_count, send_lists, slot_owner_row, prolong_blocks, prolong_cols, coarse_pattern, operator_blocks
    )

    chunk = 8
    packed = pl.pallas_call(
        functools.partial(product_kernel, n_grp, n_dom, rows, hs, ka, kp),
        grid=(total_ids // chunk,),
        out_shape=jax.ShapeDtypeStruct((total_ids, rows * BS, LANES), jnp.bfloat16),
        in_specs=[smem_spec()] * 2 + [any_spec()] * 2,
        out_specs=pl.BlockSpec((chunk, rows * BS, LANES), lambda k: (k, 0, 0)),
        scratch_shapes=[
            pltpu.VMEM((rows, ka, BS, 3 * BS), jnp.bfloat16),
            pltpu.VMEM((panel_count, BS, kp * BS), jnp.float32),
            pltpu.VMEM((panel_count, 3 * BS, kp * BS), jnp.bfloat16),
            pltpu.VMEM((total_ids, rows, BS, LANES), jnp.float32),
            sem((2,)),
        ],
        compiler_params=pltpu.CompilerParams(vmem_limit_bytes=63000 * 1024),
        name="block_products",
    )(operator_cols, meta, stacked, table)

    summed = pl.pallas_call(
        functools.partial(exchange_kernel, n_grp, n_dom, rows, hs, kp, kc, cap, row_at),
        out_shape=f32(owned, kc, BS, BS),
        in_specs=[smem_spec()] * 3 + [any_spec()] * 2,
        out_specs=vmem_spec(),
        scratch_shapes=[
            pltpu.VMEM((total_ids, rows * BS, LANES), jnp.bfloat16),
            pltpu.VMEM((rows, kp, BS, BS), jnp.float32),
            sem((2,)),
            pltpu.VMEM((used, BS, kc * BS), jnp.float32),
            pltpu.VMEM((n_dom - 1, BS, kc * BS), jnp.float32),
            pltpu.VMEM((owned, BS, kc * BS), jnp.float32),
            sem((n_dom - 1,)), sem((n_dom - 1,)),
        ],
        compiler_params=pltpu.CompilerParams(
            collective_id=1, has_side_effects=True, vmem_limit_bytes=63000 * 1024
        ),
        name="sum_rows",
    )(prolong_slot, slot_owner_row, meta, packed, prolong)
    return summed.reshape(owned, kc, BS * BS)


def solution(mesh):
    blocks = P(("grp", "dom"), None, None)
    lists = P(("grp", "dom"), None)
    return jax.shard_map(
        per_device,
        mesh=mesh,
        in_specs=(blocks, lists, P(("grp", "dom")), blocks, lists, lists, lists, lists, lists),
        out_specs=blocks,
        check_vma=False,
    )
```

```python
import functools

import jax
import jax.numpy as jnp
from jax import lax
from jax.experimental import pallas as pl
from jax.experimental.pallas import tpu as pltpu
from jax.sharding import PartitionSpec as P

BS = 64
KG = 12
KH = 4
LANES = 128


def any_spec():
    return pl.BlockSpec(memory_space=pl.ANY)


def vmem_spec():
    return pl.BlockSpec(memory_space=pltpu.VMEM)


def smem_spec():
    return pl.BlockSpec(memory_space=pltpu.SMEM)


def prepare_rows(
    n_dom, rows, hs, kp, kc, cap,
    picked, owner, prolong_raw, prolong_cols, pattern,
    panels, outgoing, prolong, dom_meta, grp_meta,
):
    owned = pattern.shape[0]
    for i in range(rows):
        raw = prolong_raw[i]
        for a in range(BS):
            prolong[i, :, a, :] = raw[:, a * BS:(a + 1) * BS]
        for q in range(0, kp, 2):
            panels[i, :, q * BS:(q + 2) * BS] = jnp.concatenate([prolong[i, q], prolong[i, q + 1]], axis=1)
    grp_meta[...] = jnp.zeros(grp_meta.shape, jnp.int32)
    dom_meta[...] = jnp.zeros(dom_meta.shape, jnp.int32)
    for i in range(rows):
        grp_meta[:, i * kp:(i + 1) * kp] = prolong_cols[i:i + 1, :]
    row_at = hs * kp + owned * kc

    def for_dom(d, carry):
        for h in range(hs):
            row = picked[0, d * hs + h]
            outgoing[d * hs + h] = panels[row]
            dom_meta[d, :, h * kp:(h + 1) * kp] = prolong_cols[pl.ds(row, 1), :]
        for r in range(owned):
            at = hs * kp + r * kc
            dom_meta[d, :, at:at + kc] = pattern[r:r + 1, :]
        dom_meta[d, :, row_at:row_at + 1] = jnp.full((1, 1), owner[0, d * cap], jnp.int32)
        return carry

    lax.fori_loop(0, n_dom, for_dom, 0)


def gather_kernel(
    n_grp, n_dom, rows, hs, kp, kc, cap,
    halo, picked, owner, prolong_raw, prolong_cols, pattern, operator_in,
    table, meta, stacked_out, prolong_out,
    operator, stacked, prolong, bulk_sem,
    panels, outgoing, dom_meta, grp_meta, blocks, own_sem, line_send, line_recv, dom_send, dom_recv, meta_send, meta_recv,
):
    g = lax.axis_index("grp")
    me = lax.axis_index("dom")
    far_base = n_grp * rows
    barrier = pltpu.get_barrier_semaphore()
    for k in range(1, n_grp):
        pl.semaphore_signal(barrier, inc=1, device_id={"grp": lax.rem(g + k, n_grp)})
    for k in range(1, n_dom):
        pl.semaphore_signal(barrier, inc=1, device_id={"dom": lax.rem(me + k, n_dom)})
    operator_copy = pltpu.make_async_copy(operator_in, operator, bulk_sem.at[0])
    operator_copy.start()
    prepare_rows(
        n_dom, rows, hs, kp, kc, cap,
        picked, owner, prolong_raw, prolong_cols, pattern,
        panels, outgoing, prolong, dom_meta, grp_meta,
    )
    pl.semaphore_wait(barrier, n_grp + n_dom - 2)

    def line_copy(direction, step, r, src, origin):
        target = g + 1 if direction == 0 else g - 1
        return pltpu.make_async_remote_copy(
            src_ref=src,
            dst_ref=table.at[origin * rows + r],
            send_sem=line_send.at[direction, step, r],
            recv_sem=line_recv.at[direction, step, r],
            device_id={"grp": target},
        )

    can_send = (g < n_grp - 1, g > 0)
    for r in range(rows):
        for direction in range(2):
            @pl.when(can_send[direction])
            def _():
                line_copy(direction, 0, r, panels.at[r], g).start()

    def meta_copy(k, over_dom):
        if over_dom:
            target = lax.rem(me + k, n_dom)
            return pltpu.make_async_remote_copy(
                src_ref=dom_meta.at[target], dst_ref=meta.at[n_grp + me],
                send_sem=meta_send.at[n_grp + k], recv_sem=meta_recv.at[n_grp + k],
                device_id={"dom": target},
            )
        return pltpu.make_async_remote_copy(
            src_ref=grp_meta, dst_ref=meta.at[g],
            send_sem=meta_send.at[k], recv_sem=meta_recv.at[k],
            device_id={"grp": lax.rem(g + k, n_grp)},
        )

    def dom_copy(k):
        target = lax.rem(me + k, n_dom)
        return pltpu.make_async_remote_copy(
            src_ref=outgoing.at[pl.ds(target * hs, hs)],
            dst_ref=table.at[pl.ds(far_base + me * hs, hs)],
            send_sem=dom_send.at[k], recv_sem=dom_recv.at[k],
            device_id={"dom": target},
        )

    for k in range(1, n_grp):
        meta_copy(k, False).start()
    for k in range(1, n_dom):
        dom_copy(k).start()
        meta_copy(k, True).start()
    own = (
        pltpu.make_async_copy(panels, table.at[pl.ds(g * rows, rows)], own_sem.at[0]),
        pltpu.make_async_copy(outgoing.at[pl.ds(me * hs, hs)], table.at[pl.ds(far_base + me * hs, hs)], own_sem.at[1]),
        pltpu.make_async_copy(grp_meta, meta.at[g], own_sem.at[2]),
        pltpu.make_async_copy(dom_meta.at[me], meta.at[n_grp + me], own_sem.at[3]),
    )
    for copy in own:
        copy.start()

    def relay_row(i, carry):
        row = operator[i]
        for a in range(BS):
            blocks[i, :, a, :] = row[:, a * BS:(a + 1) * BS]
        return carry

    def split_row(i, carry):
        for m in range(blocks.shape[1]):
            block = blocks[i, m]
            if m >= KG:
                block = jnp.where(m - KG < halo[i], block, 0.0)
            high = block.astype(jnp.bfloat16).astype(jnp.float32)
            stacked[i, m] = jnp.concatenate([high, high, block - high], axis=1).astype(jnp.bfloat16)
        return carry

    prolong_copy = pltpu.make_async_copy(prolong, prolong_out, bulk_sem.at[1])
    stacked_copy = pltpu.make_async_copy(stacked, stacked_out, bulk_sem.at[2])
    prolong_copy.start()
    operator_copy.wait()
    lax.fori_loop(0, rows, relay_row, 0)
    lax.fori_loop(0, rows, split_row, 0)
    stacked_copy.start()

    def origin_of(direction, step):
        return g - 1 - step if direction == 0 else g + 1 + step

    for step in range(n_grp - 1):
        for r in range(rows):
            for direction in range(2):
                origin = origin_of(direction, step)
                exists = (origin >= 0) & (origin < n_grp)

                @pl.when(exists)
                def _():
                    src = table.at[origin * rows + r]
                    line_copy(direction, step, r, src, origin).wait_recv()

                if step < n_grp - 2:
                    @pl.when(exists & can_send[direction])
                    def _():
                        src = table.at[origin * rows + r]
                        line_copy(direction, step + 1, r, src, origin).start()

    prolong_copy.wait()
    stacked_copy.wait()
    for copy in own:
        copy.wait()
    for k in range(1, n_grp):
        meta_copy(k, False).wait()
    for k in range(1, n_dom):
        dom_copy(k).wait()
        meta_copy(k, True).wait()
    for step in range(n_grp - 1):
        for r in range(rows):
            for direction in range(2):
                origin = g - step if direction == 0 else g + step
                exists = (origin >= 0) & (origin < n_grp)

                @pl.when(exists & can_send[direction])
                def _():
                    line_copy(direction, step, r, panels.at[r], origin).wait_send()


def split_pair(x):
    high = x.astype(jnp.bfloat16)
    low = (x - high.astype(jnp.float32)).astype(jnp.bfloat16)
    return high, low


def product_kernel(
    n_grp, n_dom, rows, hs, ka, kp,
    cols, meta,
    operator_in, table_in,
    out,
    operator, table, split_table, total, load_sem,
):
    k = pl.program_id(0)
    panel_count = table.shape[0]
    near_count = n_grp * rows
    lane = lax.broadcasted_iota(jnp.int32, (BS, LANES), 1) < BS

    @pl.when(k == 0)
    def _():
        table_copy = pltpu.make_async_copy(table_in, table, load_sem.at[0])
        operator_copy = pltpu.make_async_copy(operator_in, operator, load_sem.at[1])
        table_copy.start()
        operator_copy.start()

        def clear(e, carry):
            total[e] = jnp.zeros(total.shape[1:], jnp.float32)
            return carry

        lax.fori_loop(0, total.shape[0], clear, 0)

        def split(p, carry):
            high, low = split_pair(table[p])
            split_table[p, 0:BS] = high
            split_table[p, BS:2 * BS] = low
            split_table[p, 2 * BS:3 * BS] = high
            return carry

        table_copy.wait()
        lax.fori_loop(0, panel_count, split, 0)
        operator_copy.wait()

        def pairs(m, carry):
            near = m < KG
            products = []
            places = []
            for i in range(rows):
                col = cols[i, m]
                panel = jnp.where(near, col, near_count + col)
                meta_row = jnp.where(near, col // rows, n_grp + col // hs)
                meta_lane = jnp.where(near, (col % rows) * kp, (col % hs) * kp)
                products.append(
                    jnp.dot(operator[i, m], split_table[panel], preferred_element_type=jnp.float32)
                )
                places.append((meta_row, meta_lane))
            for i in range(rows):
                for start in range(0, kp, 4):
                    updates = []
                    for q in range(start, min(start + 4, kp), 2):
                        piece = products[i][:, q * BS:(q + 2) * BS]
                        turned = pltpu.roll(piece, BS, 1)
                        first = meta[places[i][0], 0, places[i][1] + q]
                        second = meta[places[i][0], 0, places[i][1] + q + 1]
                        updates.append((first, total[first, i] + jnp.where(lane, piece, turned)))
                        updates.append((second, total[second, i] + jnp.where(lane, turned, piece)))
                    for place, value in updates:
                        total[place, i] = value
            return carry

        lax.fori_loop(0, ka, pairs, 0)

    chunk = out.shape[0]
    half = lax.broadcasted_iota(jnp.int32, (rows * BS, LANES), 1) < BS

    def fold(t, carry):
        value = total[k * chunk + t].reshape(rows * BS, LANES)
        high = value.astype(jnp.bfloat16).astype(jnp.float32)
        out[t] = jnp.where(half, high, value - high).astype(jnp.bfloat16)
        return carry

    lax.fori_loop(0, chunk, fold, 0, unroll=4)


def exchange_kernel(
    n_grp, n_dom, rows, hs, kp, kc, cap, row_at,
    slots, owner, meta, packed_in, prolong_in,
    out,
    packed, prolong, load_sem, partial, arrived, summed, send_sem, recv_sem,
):
    me = lax.axis_index("dom")
    loads = (
        pltpu.make_async_copy(packed_in, packed, load_sem.at[0]),
        pltpu.make_async_copy(prolong_in, prolong, load_sem.at[1]),
    )
    for load in loads:
        load.start()
    barrier = pltpu.get_barrier_semaphore()
    for k in range(1, n_dom):
        pl.semaphore_signal(barrier, inc=1, device_id={"dom": lax.rem(me + k, n_dom)})
    pl.semaphore_wait(barrier, n_dom - 1)
    for load in loads:
        load.wait()
    lane = lax.broadcasted_iota(jnp.int32, (BS, LANES), 1) < BS

    def slot_rows(owner_dom, slot, at):
        owner_row = owner[0, slot]
        pattern_at = hs * kp + owner_row * kc
        left = []
        for i in range(rows):
            place = jnp.int32(kp)
            for j in range(kp):
                place = jnp.where(slots[i, j] == slot, j, place)
            block = prolong[i, jnp.minimum(place, kp - 1)]
            left.append(jnp.where(place < kp, block, 0.0).T)
        left_high, left_low = split_pair(jnp.concatenate(left, axis=1))
        both = jnp.concatenate([left_high, left_low], axis=0)
        for c in range(0, kc, 2):
            right = jnp.concatenate(
                [packed[meta[n_grp + owner_dom, 0, pattern_at + c + h]] for h in range(2)], axis=1
            )
            stacked = jnp.dot(both, right, preferred_element_type=jnp.float32)
            both_sum = stacked[:BS] + stacked[BS:]
            folded = []
            for h in range(2):
                piece = both_sum[:, h * LANES:(h + 1) * LANES]
                folded.append(piece + pltpu.roll(piece, BS, 1))
            partial[at, :, c * BS:(c + 2) * BS] = jnp.where(lane, folded[0], folded[1])

    assert n_dom & (n_dom - 1) == 0

    def partner(k):
        other = 0
        bit = 1
        while bit < n_dom:
            other += lax.rem(me // bit + k // bit, 2) * bit
            bit *= 2
        return other

    def copy_of(k):
        target = partner(k)
        return pltpu.make_async_remote_copy(
            src_ref=partial.at[k], dst_ref=arrived.at[k - 1],
            send_sem=send_sem.at[k - 1], recv_sem=recv_sem.at[k - 1],
            device_id={"dom": target},
        )

    def far_slot(step, carry):
        k = n_dom - step
        target = partner(k)
        slot_rows(target, target * cap, k)

        @pl.when(step > 1)
        def _():
            copy_of(k + 1).start()

        return carry

    lax.fori_loop(1, n_dom, far_slot, 0)
    slot_rows(me, me * cap, 0)
    copy_of(1).start()
    owned = out.shape[0]
    for r in range(owned):
        summed[r] = partial[0] * (owner[0, me * cap] == r).astype(jnp.float32)
    for t in range(1, cap):
        slot_rows(me, me * cap + t, n_dom + t - 1)
        for r in range(owned):
            summed[r] += partial[n_dom + t - 1] * (owner[0, me * cap + t] == r).astype(jnp.float32)
    for k in range(n_dom - 1, 0, -1):
        copy_of(k).wait_recv()
        source = partner(k)
        row = meta[n_grp + source, 0, row_at]
        for r in range(owned):
            summed[r] += arrived[k - 1] * (row == r).astype(jnp.float32)
    for r in range(owned):
        for c in range(kc):
            out[r, c] = summed[r, :, c * BS:(c + 1) * BS]
    for k in range(1, n_dom):
        copy_of(k).wait_send()


def per_device(
    operator_blocks, operator_cols, halo_count, prolong_blocks, prolong_cols,
    prolong_slot, send_lists, slot_owner_row, coarse_pattern,
):
    n_grp = lax.axis_size("grp")
    n_dom = lax.axis_size("dom")
    rows, ka = operator_cols.shape
    kp = prolong_cols.shape[1]
    owned, kc = coarse_pattern.shape
    hs = send_lists.shape[1] // n_dom
    cap = slot_owner_row.shape[1] // n_dom
    total_ids = owned * n_grp * n_dom
    used = n_dom + cap - 1
    panel_count = n_grp * rows + n_dom * hs
    row_at = hs * kp + owned * kc
    f32 = lambda *shape: jax.ShapeDtypeStruct(shape, jnp.float32)
    i32 = lambda *shape: jax.ShapeDtypeStruct(shape, jnp.int32)

    sem = pltpu.SemaphoreType.DMA
    table, meta, stacked, prolong = pl.pallas_call(
        functools.partial(gather_kernel, n_grp, n_dom, rows, hs, kp, kc, cap),
        out_shape=(
            f32(panel_count, BS, kp * BS), i32(n_grp + n_dom, 1, LANES),
            jax.ShapeDtypeStruct((rows, ka, BS, 3 * BS), jnp.bfloat16), f32(rows, kp, BS, BS),
        ),
        in_specs=[smem_spec()] * 3 + [vmem_spec()] * 3 + [any_spec()],
        out_specs=(any_spec(),) * 4,
        scratch_shapes=[
            pltpu.VMEM((rows, ka, BS * BS), jnp.float32),
            pltpu.VMEM((rows, ka, BS, 3 * BS), jnp.bfloat16),
            pltpu.VMEM((rows, kp, BS, BS), jnp.float32),
            sem((3,)),
            pltpu.VMEM((rows, BS, kp * BS), jnp.float32),
            pltpu.VMEM((n_dom * hs, BS, kp * BS), jnp.float32),
            pltpu.VMEM((n_dom, 1, LANES), jnp.int32),
            pltpu.VMEM((1, LANES), jnp.int32),
            pltpu.VMEM((rows, ka, BS, BS), jnp.float32),
            sem((4,)), sem((2, n_grp - 1, rows)), sem((2, n_grp - 1, rows)),
            sem((n_dom,)), sem((n_dom,)), sem((n_grp + n_dom,)), sem((n_grp + n_dom,)),
        ],
        compiler_params=pltpu.CompilerParams(collective_id=0, has_side_effects=True),
        name="gather_rows",
    )(
        halo_count, send_lists, slot_owner_row, prolong_blocks, prolong_cols, coarse_pattern, operator_blocks
    )

    chunk = 8
    packed = pl.pallas_call(
        functools.partial(product_kernel, n_grp, n_dom, rows, hs, ka, kp),
        grid=(total_ids // chunk,),
        out_shape=jax.ShapeDtypeStruct((total_ids, rows * BS, LANES), jnp.bfloat16),
        in_specs=[smem_spec()] * 2 + [any_spec()] * 2,
        out_specs=pl.BlockSpec((chunk, rows * BS, LANES), lambda k: (k, 0, 0)),
        scratch_shapes=[
            pltpu.VMEM((rows, ka, BS, 3 * BS), jnp.bfloat16),
            pltpu.VMEM((panel_count, BS, kp * BS), jnp.float32),
            pltpu.VMEM((panel_count, 3 * BS, kp * BS), jnp.bfloat16),
            pltpu.VMEM((total_ids, rows, BS, LANES), jnp.float32),
            sem((2,)),
        ],
        compiler_params=pltpu.CompilerParams(vmem_limit_bytes=63000 * 1024),
        name="block_products",
    )(operator_cols, meta, stacked, table)

    summed = pl.pallas_call(
        functools.partial(exchange_kernel, n_grp, n_dom, rows, hs, kp, kc, cap, row_at),
        out_shape=f32(owned, kc, BS, BS),
        in_specs=[smem_spec()] * 3 + [any_spec()] * 2,
        out_specs=vmem_spec(),
        scratch_shapes=[
            pltpu.VMEM((total_ids, rows * BS, LANES), jnp.bfloat16),
            pltpu.VMEM((rows, kp, BS, BS), jnp.float32),
            sem((2,)),
            pltpu.VMEM((used, BS, kc * BS), jnp.float32),
            pltpu.VMEM((n_dom - 1, BS, kc * BS), jnp.float32),
            pltpu.VMEM((owned, BS, kc * BS), jnp.float32),
            sem((n_dom - 1,)), sem((n_dom - 1,)),
        ],
        compiler_params=pltpu.CompilerParams(
            collective_id=1, has_side_effects=True, vmem_limit_bytes=63000 * 1024
        ),
        name="sum_rows",
    )(prolong_slot, slot_owner_row, meta, packed, prolong)
    return summed.reshape(owned, kc, BS * BS)


def solution(mesh):
    blocks = P(("grp", "dom"), None, None)
    lists = P(("grp", "dom"), None)
    return jax.shard_map(
        per_device,
        mesh=mesh,
        in_specs=(blocks, lists, P(("grp", "dom")), blocks, lists, lists, lists, lists, lists),
        out_specs=blocks,
        check_vma=False,
    )
```
